256 devices in a mesh: rows: 64 (over x, z, core), cols: 4 (over y).
Axes of the slice: x: 4, y: 4, z: 8, core: 2. Of those that a mesh axis runs over, the one named last changes fastest.
Arguments:
- operator_blocks: bfloat16 [8, 64, 64, 16384], P(None, None, None, 'rows'), may hold values from -0.75 to 0.75
- tentative: bfloat16 [64, 64, 16384], P(None, 'cols', 'rows'), may hold values from -1.5 to 1.5
- jacobi_scale: bfloat16 [64, 16384], P(None, 'rows'), may hold values from 0.29882812 to 1.1953125
- columns: int32 [8, 16384], P(None, 'rows'), may hold values from 0 to 16383, as said below
Outputs:
- prolongator: bfloat16 [64, 64, 16384], P(None, 'cols', 'rows')
- coarse_diag: float32 [64, 64, 16384], P('cols', None, 'rows')
- coarse_off: bfloat16 [64, 6, 64, 16384], P('cols', None, None, 'rows')
The draws below stay inside these ranges and needn't reach their ends.
Inputs may be any that keep to these rules, and one draw needn't show every extreme that they name: Rows number the elements of a periodic grid of 8 x 16 x (2 * 64) elements, first dimension fastest; each device holds 2 whole layers. columns[0, i] is i. columns[1, i] is the partner of i in a perfect matching (its partner is i again): either the neighbour of i along the first dimension on the same device, or a row on the device 64 / 2 indices away along rows, or a row on the device whose index along rows differs in the lowest bit. columns[2 .. 7, i] are the six face neighbours of i, in the order minus first, plus first, minus second, plus second, minus third, plus third dimension. `columns`: for two different devices along rows, the pairs with one row on each number either zero or exactly 2; every draw has such a pair of devices with 2.
All inputs are finite; a program needn't handle non-finite values.
Results may differ from the reference program's by a relative error of at most 0.0064.
Values may be sent and summed in bfloat16 or wider, within the bound.
A program may use at most 192 MiB of HBM per device.

```python
import math
import jax
import jax.numpy as jnp
from jax import lax

BS = 64
SLOTS = 8
GX = 8
GY = 16
R_DEV = 256
CAP = 2
SLAB = 16384


def draw_columns(key, part):
    ndev = SLAB // R_DEV
    half_dev = ndev // 2
    pair_dev = ndev // 2
    plane = GX * GY
    layers = R_DEV // plane
    half_x = GX // 2
    half_y = GY // 2
    npairs = half_x * half_y
    keys = jax.random.split(jax.random.fold_in(key, 7), 4)
    row_ids = jnp.arange(SLAB, dtype=jnp.int32)
    xpos = row_ids % GX
    ypos = row_ids // GX % GY
    zpos = row_ids // plane
    device_of = zpos // layers
    level = zpos % layers
    active_far = jax.random.randint(keys[0], (half_dev,), 0, 2) == 1
    active_far = active_far | (jnp.arange(half_dev) == 0)
    active_near = jax.random.randint(keys[2], (pair_dev,), 0, 2) == 1
    active_near = active_near | (jnp.arange(pair_dev) == 0)
    shuffles_far = jax.vmap(lambda sub_key: jax.random.permutation(sub_key, npairs))(jax.random.split(keys[1], half_dev))
    shuffles_near = jax.vmap(lambda sub_key: jax.random.permutation(sub_key, npairs))(jax.random.split(keys[3], pair_dev))
    chosen_far = jnp.argsort(shuffles_far, axis=1) < CAP // 2
    chosen_near = jnp.argsort(shuffles_near, axis=1) < CAP // 2
    low_y = ypos < half_y
    index_far = jnp.clip(xpos // 2 + half_x * ypos, 0, npairs - 1)
    index_near = jnp.clip(xpos // 2 + half_x * (ypos - half_y), 0, npairs - 1)
    low_half = device_of < half_dev
    base_dev = jnp.where(low_half, device_of, device_of - half_dev)
    group_dev = device_of // 2
    crossing_far = (level == 0) & low_y & active_far[base_dev] & chosen_far[base_dev, index_far]
    crossing_near = (level == 0) & ~low_y & active_near[group_dev] & chosen_near[group_dev, index_near]
    base = row_ids - xpos - ypos * GX
    minus_x = base + (xpos - 1) % GX + ypos * GX
    plus_x = base + (xpos + 1) % GX + ypos * GX
    minus_y = base + xpos + (ypos - 1) % GY * GX
    plus_y = base + xpos + (ypos + 1) % GY * GX
    minus_z = (row_ids - plane) % SLAB
    plus_z = (row_ids + plane) % SLAB
    faces = jnp.stack([minus_x, plus_x, minus_y, plus_y, minus_z, plus_z], axis=0)
    local_mate = jnp.where(xpos % 2 == 0, plus_x, minus_x)
    far_mate = row_ids + jnp.where(low_half, half_dev, -half_dev) * R_DEV
    near_mate = row_ids + jnp.where(device_of % 2 == 0, 1, -1) * R_DEV
    partner = jnp.where(crossing_far, far_mate, jnp.where(crossing_near, near_mate, local_mate))
    return jnp.concatenate([row_ids[None, :], partner[None, :], faces], axis=0).astype(jnp.int32)


def steps_of(own_key, shape, pieces, smallest, largest):
    gain = 1.0
    for dim, parts in pieces:
        heights = jax.random.uniform(jax.random.fold_in(jax.random.fold_in(own_key, 6), dim), (parts,), jnp.float32, smallest / len(pieces), largest / len(pieces))
        gain = gain * jnp.repeat(jnp.exp(heights), shape[dim] // parts).reshape((-1,) + (1,) * (len(shape) - 1 - dim))
    return gain


def centred(own_key, shape, scale, bound, pieces=(), held_as=jnp.bfloat16):
    level = steps_of(own_key, shape, pieces, -0.22, 0.18) if pieces else 1.0
    result = jax.random.normal(own_key, shape, jnp.float32) * scale * level
    return jnp.minimum(jnp.maximum(result, -bound), bound).astype(held_as)


def setup_inputs(seed: int = 0) -> dict:
    key_of = jax.random.split(jax.random.key(seed), 5)
    operator_blocks = centred(key_of[0], (SLOTS, BS, BS, SLAB), BS ** -0.5, 0.75, ((3, 64),))
    tentative = centred(key_of[1], (BS, BS, SLAB), 0.25, 1.5, ((1, 4), (2, 64)))
    jacobi_scale = jnp.clip(jnp.exp(math.log(1.1953125) - 1.3862944 * jax.random.uniform(key_of[2], (BS, SLAB), jnp.float32) ** steps_of(key_of[2], (BS, SLAB), ((1, 64),), -0.2, 0.2)), 0.29882812, 1.1953125).astype(jnp.bfloat16)
    columns = draw_columns(jax.random.fold_in(key_of[4], 71), 0)
    return dict(operator_blocks=operator_blocks, tentative=tentative, jacobi_scale=jacobi_scale, columns=columns)


def block_product(left_blocks, right_blocks):
    return jnp.einsum("fgx,gcx->fcx", left_blocks.astype(jnp.float32), right_blocks.astype(jnp.float32))


def reference(operator_blocks, tentative, jacobi_scale, columns):
    partner = columns[1]
    tent_other = jnp.take(tentative, partner, axis=2)
    coupled = block_product(operator_blocks[0], tentative) + block_product(operator_blocks[1], tent_other)
    prolongator = (tentative.astype(jnp.float32) - jacobi_scale.astype(jnp.float32)[:, None, :] * coupled).astype(jnp.bfloat16)
    left_wide = prolongator.astype(jnp.float32)

    def slot_term(slot_id):
        right_blocks = jnp.take(prolongator, columns[slot_id], axis=2)
        reached = block_product(operator_blocks[slot_id], right_blocks).astype(jnp.bfloat16)
        reached = lax.optimization_barrier(reached).astype(jnp.float32)
        return jnp.einsum("fax,fcx->cax", left_wide, reached)

    own_sum = slot_term(0) + slot_term(1)
    coarse_diag = own_sum + jnp.take(own_sum, partner, axis=2)
    off_terms = lax.map(lambda slot_id: slot_term(slot_id).astype(jnp.bfloat16), jnp.arange(2, SLOTS, dtype=jnp.int32))
    coarse_off = jnp.transpose(off_terms, (1, 0, 2, 3))
    return prolongator, coarse_diag, coarse_off
```

```python
import functools

import jax
import jax.numpy as jnp
from jax import lax
from jax.experimental import pallas as pl
from jax.experimental.pallas import tpu as pltpu
from jax.sharding import PartitionSpec as P

GX = 8
GY = 16
LAYER = GX * GY
BS = 64
PART = 16
STRIDE = LAYER + 8
CSTRIDE = 392
BIG = 1 << 20
MESH = pl.DeviceIdType.MESH
F32 = jnp.float32
BF16 = jnp.bfloat16
NT = (((1,), (1,)), ((), ()))
TN = (((0,), (0,)), ((), ()))


def iota(shape, dim):
    return lax.broadcasted_iota(jnp.int32, shape, dim)


def group_rows(block):
    return pl.ds(pl.multiple_of(block * STRIDE, 8), LAYER)


def of_position(position):
    return pl.ds(position, BS, stride=STRIDE)


def loop(count, unroll, body):
    def step(index, carry):
        for inner in range(unroll):
            body(index * unroll + inner)
        return carry

    lax.fori_loop(0, count // unroll, step, 0)


def relay(stage, target):
    def body(fine):
        for half in range(2):
            block = stage[:, fine, :, half * LAYER : (half + 1) * LAYER].reshape(128, LAYER)
            target[half, group_rows(fine), :] = block.T.astype(F32)

    loop(BS, 8, body)


def spread(rows_of, target):
    def body(fine):
        target[group_rows(fine), :] = jnp.concatenate(rows_of(fine), axis=0).T.astype(F32)

    loop(BS, 8, body)


def halves(ref, index):
    return ref[index, :, :LAYER], ref[index, :, LAYER:]


def left_of(ax, pair, position):
    return jnp.concatenate(
        [ax[pair, half, of_position(position), :] for half in range(2)], axis=0
    ).astype(BF16)


def pick_plan(columns, device, far, near):
    count = columns.shape[1]
    partner = columns[1:2, :]
    row = iota((1, count), 1).astype(F32)
    value = partner.astype(F32)
    perm = (iota((count, count), 0) == partner - device * count).astype(BF16)
    order = iota((PART, count), 0)
    send, take = [], []
    for other in (far, near):
        there = (partner >= other * count) & (partner < (other + 1) * count)
        for entry, found in ((row, send), (value, take)):
            first = jnp.min(jnp.where(there, entry, float(BIG)), axis=1, keepdims=True)
            last = jnp.max(jnp.where(there, entry, -1.0), axis=1, keepdims=True)
            wanted = jnp.where(order == 0, first, jnp.where(order == 1, last, -2.0))
            hit = jnp.where(there, entry, -3.0) == wanted
            found.append(hit.astype(F32).astype(BF16))
    return perm, jnp.concatenate(send, axis=0), jnp.concatenate(take, axis=0)


def kernel(
    a_hbm, t_ref, s_ref, col_ref, p_out, d_out, o_out,
    stage, ax, pn, yx, rr, pxl, other, pc, gath, below, above, xf, own, s32, plan_perm, plan_send,
    plan_take, snd, rcv, in_sem, out_sem, send_sem, recv_sem,
):
    device = lax.axis_index("rows")
    part = lax.axis_index("cols")
    devices = lax.axis_size("rows")
    parts = lax.axis_size("cols")
    far = lax.rem(device + devices // 2, devices)
    near = device + 1 - 2 * lax.rem(device, 2)
    up = lax.rem(device + 1, devices)
    down = lax.rem(device + devices - 1, devices)
    right = lax.rem(part + 1, parts)
    left = lax.rem(part + parts - 1, parts)
    opposite = lax.rem(part + 2, parts)

    def fetch(pair, slot):
        return pltpu.make_async_copy(a_hbm.at[pl.ds(2 * pair, 2)], stage.at[slot], in_sem.at[slot])

    def send(source, target, index, to):
        return pltpu.make_async_remote_copy(
            src_ref=source, dst_ref=target, send_sem=send_sem.at[index],
            recv_sem=recv_sem.at[index], device_id=to, device_id_type=MESH,
        )

    def exchange(turn):
        return [
            send(snd.at[turn, kind], rcv.at[turn, kind], 2 * turn + kind, (who, part))
            for kind, who in ((0, far), (1, near))
        ]

    fetch(0, 0).start()
    fetch(1, 1).start()
    barrier = pltpu.get_barrier_semaphore()
    for who in ((far, part), (up, part), (down, part), (device, right), (device, left)):
        pl.semaphore_signal(barrier, inc=1, device_id=who, device_id_type=MESH)

    perm, send_rows, take_rows = pick_plan(col_ref, device, far, near)
    plan_perm[...] = perm
    plan_send[...] = send_rows
    plan_take[...] = take_rows
    for half in range(2):
        s32[half] = s_ref[:, half * LAYER : (half + 1) * LAYER].astype(F32)

    def pack(turn, matrix):
        rows = lax.dot_general(plan_send[...], matrix, NT, preferred_element_type=F32).astype(BF16)
        snd[turn, 0] = rows[:PART]
        snd[turn, 1] = rows[PART:]

    def arrived(turn):
        rows = rcv[turn].reshape(2 * PART, -1)
        return lax.dot_general(rows, plan_take[...], TN, preferred_element_type=F32)

    pack(0, t_ref[...].reshape(BS * PART, 2 * LAYER))
    pl.semaphore_wait(barrier, 5)
    first = exchange(0)
    for copy in first:
        copy.start()

    fetch(0, 0).wait()
    relay(stage.at[0], ax.at[0])
    fetch(2, 0).start()

    for copy in first:
        copy.wait()
    moved = jnp.dot(
        t_ref[...].reshape(BS * PART, 2 * LAYER), plan_perm[...], preferred_element_type=F32
    )
    other[...] = (moved + arrived(0)).astype(BF16).reshape(BS, PART, 2 * LAYER)

    tt = ax.at[1, 0]
    cp = ax.at[1, 1]
    spread(lambda fine: [*halves(t_ref, fine), *halves(other, fine)] * 2, tt)

    lane = iota((1, 128), 1)
    mask = [((lane >= 32 * j) & (lane < 32 * j + 32)).astype(F32).astype(BF16) for j in range(4)]
    own_low = ((lane & 63) < 32).astype(F32).astype(BF16)
    own_high = ((lane & 63) >= 32).astype(F32).astype(BF16)
    first_layer = (iota((BS, 128), 1) & 16) == 0
    keep = ((iota((128, 128), 1) & 16) == 0) == (iota((128, 128), 0) < BS)

    def smooth(position):
        block = tt[of_position(position), :].astype(BF16)
        right_side = jnp.concatenate([block * own_low, block * own_high], axis=0)
        result = jnp.dot(left_of(ax, 0, position), right_side, preferred_element_type=F32)
        cp[of_position(position), :] = jnp.where(first_layer, result[:BS], result[BS:])

    loop(LAYER, 8, smooth)

    def back(pair):
        fine = 2 * pair
        joined = jnp.where(
            iota((LAYER, 128), 1) < 64, cp[group_rows(fine), :], cp[group_rows(fine + 1), :]
        ).T
        for step in range(2):
            for half in range(2):
                base = 64 * step + 16 * half
                coupled = joined[base : base + 16] + joined[base + 32 : base + 48]
                lanes = pl.ds(half * LAYER, LAYER)
                value = t_ref[fine + step, :, lanes].astype(F32)
                value = value - s32[half, pl.ds(fine + step, 1), :] * coupled
                value = value.astype(BF16)
                pxl[fine + step, :, lanes] = value
                rows = pl.ds(pl.multiple_of((fine + step) * PART, 8), PART)
                xf[half, rows, :] = value.astype(F32)

    loop(BS // 2, 4, back)

    def swap(coarse):
        for half in range(2):
            rows = xf[half, pl.ds(coarse, BS, stride=PART), :]
            pc[coarse, :, half * LAYER : (half + 1) * LAYER] = rows.astype(BF16)

    loop(PART, 4, swap)
    pack(1, pxl[...].reshape(BS * PART, 2 * LAYER))

    around = [
        send(pc, gath.at[0], 6, (device, right)),
        send(pc, gath.at[1], 7, (device, left)),
    ]
    halo = [
        send(pxl.at[:, :, pl.ds(LAYER, LAYER)], below, 8, (up, part)),
        send(pxl.at[:, :, pl.ds(0, LAYER)], above, 9, (down, part)),
    ]
    second = exchange(1)
    for copy in (*around, *halo, *second):
        copy.start()
    p_copy = pltpu.make_async_copy(pxl, p_out, out_sem.at[0])
    p_copy.start()

    spread(lambda fine: [*halves(pxl, fine)] * 4, yx)

    def settle(position):
        pn[position] = yx[of_position(position), :].astype(BF16)

    loop(LAYER, 8, settle)
    fetch(1, 1).wait()
    relay(stage.at[1], ax.at[1])
    fetch(3, 1).start()
    fetch(2, 0).wait()
    relay(stage.at[0], ax.at[2])

    def reach(slot, pairs, blocks, position):
        left_side = jnp.concatenate([left_of(ax, pair, position) for pair in pairs], axis=1)
        right_side = jnp.concatenate([block * m for block, m in zip(blocks, mask)], axis=0)
        result = jnp.dot(left_side, right_side, preferred_element_type=F32)
        rr[slot, position] = jnp.where(keep, result, 0.0).astype(BF16)

    def local_line(line, carry):
        before = lax.rem(line + GY - 1, GY) * GX
        after = lax.rem(line + 1, GY) * GX
        base = line * GX
        for x in range(GX):
            blocks = [
                pn[base + (x + GX - 1) % GX], pn[base + (x + 1) % GX], pn[before + x], pn[after + x]
            ]
            reach(0, (1, 2), blocks, base + x)
        return carry

    lax.fori_loop(0, GY, local_line, 0)

    for copy in around:
        copy.wait()
    middle = PART // 2
    relays = [
        send(gath.at[0, pl.ds(0, middle)], gath.at[2, pl.ds(0, middle)], 10, (device, right)),
        send(
            gath.at[1, pl.ds(middle, middle)], gath.at[2, pl.ds(middle, middle)], 11, (device, left)
        ),
    ]
    for copy in relays:
        copy.start()

    fetch(3, 1).wait()
    relay(stage.at[1], ax.at[1])
    for copy in second:
        copy.wait()
    moved = jnp.dot(
        pxl[...].reshape(BS * PART, 2 * LAYER), plan_perm[...], preferred_element_type=F32
    )
    other[...] = (moved + arrived(1)).astype(BF16).reshape(BS, PART, 2 * LAYER)
    for copy in halo:
        copy.wait()

    def outer_rows(fine):
        low, high = halves(pxl, fine)
        return [low, high, *halves(other, fine), below[fine], low, high, above[fine]]

    spread(outer_rows, yx)

    def remote_row(position):
        block = yx[of_position(position), :].astype(BF16)
        reach(1, (0, 1), [block] * 4, position)

    loop(LAYER, 8, remote_row)

    pf = ax.at[2, 0]

    def wide(source, index, owner):
        def body(coarse):
            block = source[coarse] if index is None else source[index, coarse]
            rows = jnp.concatenate([block[:, :LAYER], block[:, LAYER:]], axis=0)
            pf[group_rows(owner * PART + coarse), :] = rows.T.astype(F32)

        loop(PART, 8, body)

    wide(pc, None, part)
    wide(gath, 0, left)
    wide(gath, 1, right)
    for copy in relays:
        copy.wait()
    wide(gath, 2, opposite)

    def product(position):
        left_side = pf[of_position(position), :].astype(BF16)
        right_side = jnp.concatenate([rr[0, position], rr[1, position]], axis=1)
        result = jnp.dot(left_side, right_side, preferred_element_type=F32)
        for slot in range(2):
            ax[0, slot, of_position(position), :] = result[:, slot * 128 : (slot + 1) * 128]

    loop(LAYER, 8, product)

    def keep_off(slot, half, coarse_row, rows):
        start = slot * BS + coarse_row
        ax[1, half, pl.ds(start, PART, stride=CSTRIDE), :] = rows

    def finish_outer(coarse_row):
        turned = ax[0, 1, group_rows(coarse_row), :].T
        for half in range(2):
            rows = [turned[32 * j + 16 * half : 32 * j + 16 * half + 16] for j in range(4)]
            own[half, pl.ds(coarse_row, PART, stride=BS), :] = rows[0] + rows[1]
            keep_off(4, half, coarse_row, rows[2])
            keep_off(5, half, coarse_row, rows[3])

    loop(BS, 4, finish_outer)

    high = jnp.concatenate([own[0], own[1]], axis=1).astype(BF16)
    pack(2, high)
    third = exchange(2)
    for copy in third:
        copy.start()

    def finish_local(coarse_row):
        turned = ax[0, 0, group_rows(coarse_row), :].T
        for half in range(2):
            for j in range(4):
                keep_off(j, half, coarse_row, turned[32 * j + 16 * half : 32 * j + 16 * half + 16])

    loop(BS, 4, finish_local)

    def narrow(coarse):
        for slot in range(6):
            for half in range(2):
                start = pl.multiple_of(coarse * CSTRIDE + slot * BS, 8)
                plane = coarse * 6 + slot
                stage[0, plane // BS, lax.rem(plane, BS), :, half * LAYER : (half + 1) * LAYER] = ax[
                    1, half, pl.ds(start, BS), :
                ].astype(BF16)

    loop(PART, 1, narrow)
    o_copies = [
        pltpu.make_async_copy(stage.at[0, 0], o_out.at[pl.ds(0, BS)], out_sem.at[1]),
        pltpu.make_async_copy(
            stage.at[0, 1, pl.ds(0, 6 * PART - BS)], o_out.at[pl.ds(BS, 6 * PART - BS)], out_sem.at[2]
        ),
    ]
    for copy in o_copies:
        copy.start()

    whole = jnp.concatenate([own[0], own[1]], axis=1)
    high = whole.astype(BF16)
    low = (whole - high.astype(F32)).astype(BF16)
    total = whole + jnp.dot(high, plan_perm[...], preferred_element_type=F32)
    total = total + jnp.dot(low, plan_perm[...], preferred_element_type=F32)
    for copy in third:
        copy.wait()
    total = total + arrived(2)
    for half in range(2):
        own[half] = total[:, half * LAYER : (half + 1) * LAYER]
    d_copies = [
        pltpu.make_async_copy(own.at[half], d_out.at[:, pl.ds(half * LAYER, LAYER)], out_sem.at[3 + half])
        for half in range(2)
    ]
    for copy in d_copies:
        copy.start()
    for copy in (p_copy, *o_copies, *d_copies):
        copy.wait()


def on_device(operator_blocks, tentative, jacobi_scale, columns):
    rows = columns.shape[1]
    vmem = pl.BlockSpec(memory_space=pltpu.VMEM)
    hbm = pl.BlockSpec(memory_space=pl.ANY)
    prolongator, diag, off = pl.pallas_call(
        kernel,
        out_shape=(
            jax.ShapeDtypeStruct((BS, PART, rows), BF16),
            jax.ShapeDtypeStruct((PART * BS, rows), F32),
            jax.ShapeDtypeStruct((PART * 6, BS, rows), BF16),
        ),
        in_specs=[hbm, vmem, vmem, vmem],
        out_specs=(hbm, hbm, hbm),
        scratch_shapes=[
            pltpu.VMEM((2, 2, BS, BS, rows), BF16),
            pltpu.VMEM((3, 2, BS * STRIDE, 128), F32),
            pltpu.VMEM((LAYER, BS, 128), BF16),
            pltpu.VMEM((BS * STRIDE, 128), F32),
            pltpu.VMEM((2, LAYER, 128, 128), BF16),
            pltpu.VMEM((BS, PART, rows), BF16),
            pltpu.VMEM((BS, PART, rows), BF16),
            pltpu.VMEM((PART, BS, rows), BF16),
            pltpu.VMEM((3, PART, BS, rows), BF16),
            pltpu.VMEM((BS, PART, LAYER), BF16),
            pltpu.VMEM((BS, PART, LAYER), BF16),
            pltpu.VMEM((2, BS * PART, LAYER), F32),
            pltpu.VMEM((2, BS * PART, LAYER), F32),
            pltpu.VMEM((2, BS, LAYER), F32),
            pltpu.VMEM((rows, rows), BF16),
            pltpu.VMEM((2 * PART, rows), BF16),
            pltpu.VMEM((2 * PART, rows), BF16),
            pltpu.VMEM((3, 2, PART, BS * PART), BF16),
            pltpu.VMEM((3, 2, PART, BS * PART), BF16),
            pltpu.SemaphoreType.DMA((2,)),
            pltpu.SemaphoreType.DMA((5,)),
            pltpu.SemaphoreType.DMA((12,)),
            pltpu.SemaphoreType.DMA((12,)),
        ],
        compiler_params=pltpu.CompilerParams(
            collective_id=0, has_side_effects=True, vmem_limit_bytes=60 * 2**20
        ),
    )(operator_blocks, tentative, jacobi_scale, columns)
    return prolongator, diag.reshape(PART, BS, rows), off.reshape(PART, 6, BS, rows)


def solution(mesh):
    placed = (
        P(None, None, None, "rows"),
        P(None, "cols", "rows"),
        P(None, "rows"),
        P(None, "rows"),
    )
    return jax.shard_map(
        on_device,
        mesh=mesh,
        in_specs=placed,
        out_specs=(P(None, "cols", "rows"), P("cols", None, "rows"), P("cols", None, None, "rows")),
        check_vma=False,
    )
```

```python
import functools

import jax
import jax.numpy as jnp
from jax import lax
from jax.experimental import pallas as pl
from jax.experimental.pallas import tpu as pltpu
from jax.sharding import PartitionSpec as P

GX = 8
GY = 16
LAYER = GX * GY
BS = 64
PART = 16
STRIDE = LAYER + 4
CSTRIDE = 388
OSTRIDE = BS + 4
XSTRIDE = PART + 4
BIG = 1 << 20
MESH = pl.DeviceIdType.MESH
F32 = jnp.float32
BF16 = jnp.bfloat16
NT = (((1,), (1,)), ((), ()))
TN = (((0,), (0,)), ((), ()))


def iota(shape, dim):
    return lax.broadcasted_iota(jnp.int32, shape, dim)


def group_rows(block):
    return pl.ds(block * STRIDE, LAYER)


def of_position(position):
    return pl.ds(position, BS, stride=STRIDE)


def loop(count, unroll, body):
    def step(index, carry):
        for inner in range(unroll):
            body(index * unroll + inner)
        return carry

    lax.fori_loop(0, count // unroll, step, 0)


def relay_one(stage, targets, fine):
    for half in range(2):
        block = stage[:, fine, :, half * LAYER : (half + 1) * LAYER].reshape(128, LAYER)
        targets[half][group_rows(fine), :] = block.T.astype(F32)


def relay(stage, targets):
    loop(BS, 8, lambda fine: relay_one(stage, targets, fine))


def spread(rows_of, target):
    def body(fine):
        target[group_rows(fine), :] = jnp.concatenate(rows_of(fine), axis=0).T.astype(F32)

    loop(BS, 8, body)


def halves(ref, index):
    return ref[index, :, :LAYER], ref[index, :, LAYER:]


def left_of(sources, position):
    return jnp.concatenate(
        [source[of_position(position), :] for source in sources], axis=0
    ).astype(BF16)


def pick_plan(columns, device, far, near):
    count = columns.shape[1]
    partner = columns[1:2, :]
    row = iota((1, count), 1).astype(F32)
    value = partner.astype(F32)
    perm = (iota((count, count), 0) == partner - device * count).astype(BF16)
    order = iota((PART, count), 0)
    send, take = [], []
    for other in (far, near):
        there = (partner >= other * count) & (partner < (other + 1) * count)
        for entry, found in ((row, send), (value, take)):
            first = jnp.min(jnp.where(there, entry, float(BIG)), axis=1, keepdims=True)
            last = jnp.max(jnp.where(there, entry, -1.0), axis=1, keepdims=True)
            wanted = jnp.where(order == 0, first, jnp.where(order == 1, last, -2.0))
            hit = jnp.where(there, entry, -3.0) == wanted
            found.append(hit.astype(F32).astype(BF16))
    return perm, jnp.concatenate(send, axis=0), jnp.concatenate(take, axis=0)


def kernel(
    a_hbm, t_ref, s_ref, col_ref, pxl, xf, b2, b3,
    stage, b0, b1, b4, b5, b6, pn, yx, rr, other, pc, gath, below, above, own, s32, plan_perm, plan_send,
    plan_take, snd, rcv, in_sem, chunk_sem, send_sem, recv_sem,
):
    device = lax.axis_index("rows")
    part = lax.axis_index("cols")
    devices = lax.axis_size("rows")
    parts = lax.axis_size("cols")
    far = lax.rem(device + devices // 2, devices)
    near = device + 1 - 2 * lax.rem(device, 2)
    up = lax.rem(device + 1, devices)
    down = lax.rem(device + devices - 1, devices)
    right = lax.rem(part + 1, parts)
    left = lax.rem(part + parts - 1, parts)
    opposite = lax.rem(part + 2, parts)

    def fetch(pair, slot):
        return pltpu.make_async_copy(a_hbm.at[pl.ds(2 * pair, 2)], stage.at[slot], in_sem.at[slot])

    def send(source, target, index, to):
        return pltpu.make_async_remote_copy(
            src_ref=source, dst_ref=target, send_sem=send_sem.at[index],
            recv_sem=recv_sem.at[index], device_id=to, device_id_type=MESH,
        )

    def exchange(turn):
        return [
            send(snd.at[turn, kind], rcv.at[turn, kind], 2 * turn + kind, (who, part))
            for kind, who in ((0, far), (1, near))
        ]

    def first_fetch(chunk):
        rows = pl.ds(chunk * 16, 16)
        return pltpu.make_async_copy(
            a_hbm.at[pl.ds(0, 2), rows], stage.at[0, :, rows], chunk_sem.at[chunk]
        )

    for chunk in range(4):
        first_fetch(chunk).start()
    fetch(1, 1).start()
    barrier = pltpu.get_barrier_semaphore()
    for who in ((far, part), (up, part), (down, part), (device, right), (device, left)):
        pl.semaphore_signal(barrier, inc=1, device_id=who, device_id_type=MESH)

    perm, send_rows, take_rows = pick_plan(col_ref, device, far, near)
    plan_perm[...] = perm
    plan_send[...] = send_rows
    plan_take[...] = take_rows
    for half in range(2):
        s32[half] = s_ref[:, half * LAYER : (half + 1) * LAYER].astype(F32)

    def pack(turn, matrix):
        rows = lax.dot_general(plan_send[...], matrix, NT, preferred_element_type=F32).astype(BF16)
        snd[turn, 0] = rows[:PART]
        snd[turn, 1] = rows[PART:]

    def arrived(turn):
        rows = rcv[turn].reshape(2 * PART, -1)
        return lax.dot_general(rows, plan_take[...], TN, preferred_element_type=F32)

    pack(0, t_ref[...].reshape(BS * PART, 2 * LAYER))
    pl.semaphore_wait(barrier, 5)
    first = exchange(0)
    for copy in first:
        copy.start()

    for chunk in range(4):
        first_fetch(chunk).wait()
        loop(16, 8, lambda fine: relay_one(stage.at[0], (b0, b1), 16 * chunk + fine))
    fetch(2, 0).start()

    for copy in first:
        copy.wait()
    moved = jnp.dot(
        t_ref[...].reshape(BS * PART, 2 * LAYER), plan_perm[...], preferred_element_type=F32
    )
    other[...] = (moved + arrived(0)).astype(BF16).reshape(BS, PART, 2 * LAYER)

    tt, cp = yx, b6
    spread(lambda fine: [*halves(t_ref, fine), *halves(other, fine)] * 2, tt)

    lane = iota((1, 128), 1)
    mask = [((lane >= 32 * j) & (lane < 32 * j + 32)).astype(F32).astype(BF16) for j in range(4)]
    own_low = ((lane & 63) < 32).astype(F32).astype(BF16)
    own_high = ((lane & 63) >= 32).astype(F32).astype(BF16)
    first_layer = (iota((BS, 128), 1) & 16) == 0
    keep = ((iota((128, 128), 1) & 16) == 0) == (iota((128, 128), 0) < BS)

    def smooth(position):
        block = tt[of_position(position), :].astype(BF16)
        right_side = jnp.concatenate([block * own_low, block * own_high], axis=0)
        result = jnp.dot(left_of((b0, b1), position), right_side, preferred_element_type=F32)
        cp[of_position(position), :] = jnp.where(first_layer, result[:BS], result[BS:])

    loop(LAYER, 8, smooth)

    def back(pair):
        fine = 2 * pair
        joined = jnp.where(
            iota((LAYER, 128), 1) < 64, cp[group_rows(fine), :], cp[group_rows(fine + 1), :]
        ).T
        for step in range(2):
            for half in range(2):
                base = 64 * step + 16 * half
                coupled = joined[base : base + 16] + joined[base + 32 : base + 48]
                lanes = pl.ds(half * LAYER, LAYER)
                value = t_ref[fine + step, :, lanes].astype(F32)
                value = value - s32[half, pl.ds(fine + step, 1), :] * coupled
                value = value.astype(BF16)
                pxl[fine + step, :, lanes] = value
                rows = pl.ds((fine + step) * XSTRIDE, PART)
                xf[half, rows, :] = value.astype(F32)

    loop(BS // 2, 4, back)

    def swap(coarse):
        for half in range(2):
            rows = xf[half, pl.ds(coarse, BS, stride=XSTRIDE), :]
            pc[coarse, :, half * LAYER : (half + 1) * LAYER] = rows.astype(BF16)

    loop(PART, 4, swap)
    pack(1, pxl[...].reshape(BS * PART, 2 * LAYER))

    middle = PART // 2
    low = pl.ds(0, middle)
    high = pl.ds(middle, middle)
    first_half = [
        send(pc.at[low], gath.at[0, low], 6, (device, right)),
        send(pc.at[high], gath.at[1, high], 7, (device, left)),
    ]
    second_half = [
        send(pc.at[high], gath.at[0, high], 12, (device, right)),
        send(pc.at[low], gath.at[1, low], 13, (device, left)),
    ]
    relays = [
        send(gath.at[0, low], gath.at[2, low], 10, (device, right)),
        send(gath.at[1, high], gath.at[2, high], 11, (device, left)),
    ]
    halo = [
        send(pxl.at[:, :, pl.ds(LAYER, LAYER)], below, 8, (up, part)),
        send(pxl.at[:, :, pl.ds(0, LAYER)], above, 9, (down, part)),
    ]
    second = exchange(1)
    for copy in (*second, *first_half, *halo, *second_half):
        copy.start()

    spread(lambda fine: [*halves(pxl, fine)] * 4, yx)

    def settle(position):
        pn[position] = yx[of_position(position), :].astype(BF16)

    loop(LAYER, 8, settle)
    fetch(1, 1).wait()
    relay(stage.at[1], (b2, b3))
    fetch(3, 1).start()
    fetch(2, 0).wait()
    relay(stage.at[0], (b4, b5))
    for copy in first_half:
        copy.wait_recv()
    for copy in relays:
        copy.start()
    fetch(3, 1).wait()

    def reach(slot, pairs, blocks, position):
        left_side = jnp.concatenate([left_of(pair, position) for pair in pairs], axis=1)
        right_side = jnp.concatenate([block * m for block, m in zip(blocks, mask)], axis=0)
        result = jnp.dot(left_side, right_side, preferred_element_type=F32)
        rr[slot, position] = jnp.where(keep, result, 0.0).astype(BF16)

    def local_line(line, carry):
        before = lax.rem(line + GY - 1, GY) * GX
        after = lax.rem(line + 1, GY) * GX
        base = line * GX
        for x in range(GX):
            blocks = [
                pn[base + (x + GX - 1) % GX], pn[base + (x + 1) % GX], pn[before + x], pn[after + x]
            ]
            reach(0, ((b2, b3), (b4, b5)), blocks, base + x)
        for inner in range(4):
            relay_one(stage.at[1], (b6, yx), line * 4 + inner)
        return carry

    lax.fori_loop(0, GY, local_line, 0)

    for copy in second:
        copy.wait()
    moved = jnp.dot(
        pxl[...].reshape(BS * PART, 2 * LAYER), plan_perm[...], preferred_element_type=F32
    )
    other[...] = (moved + arrived(1)).astype(BF16).reshape(BS, PART, 2 * LAYER)
    for copy in halo:
        copy.wait()

    def outer_rows(fine):
        low, high = halves(pxl, fine)
        return [low, high, *halves(other, fine), below[fine], low, high, above[fine]]

    spread(outer_rows, b2)

    def remote_row(position):
        block = b2[of_position(position), :].astype(BF16)
        reach(1, ((b0, b1), (b6, yx)), [block] * 4, position)

    loop(LAYER, 8, remote_row)

    pf, off = b4, (b2, b3)

    def wide(source, index, owner):
        def body(coarse):
            block = source[coarse] if index is None else source[index, coarse]
            rows = jnp.concatenate([block[:, :LAYER], block[:, LAYER:]], axis=0)
            pf[group_rows(owner * PART + coarse), :] = rows.T.astype(F32)

        loop(PART, 8, body)

    wide(pc, None, part)
    for copy in first_half:
        copy.wait_send()
    for copy in second_half:
        copy.wait()
    wide(gath, 0, left)
    wide(gath, 1, right)
    for copy in relays:
        copy.wait()
    wide(gath, 2, opposite)

    def product(position):
        left_side = pf[of_position(position), :].astype(BF16)
        right_side = jnp.concatenate([rr[0, position], rr[1, position]], axis=1)
        result = jnp.dot(left_side, right_side, preferred_element_type=F32)
        b0[of_position(position), :] = result[:, :128]
        b1[of_position(position), :] = result[:, 128:]

    loop(LAYER, 8, product)

    def keep_off(slot, half, coarse_row, rows):
        start = slot * BS + coarse_row
        off[half][pl.ds(start, PART, stride=CSTRIDE), :] = rows

    def finish_outer(coarse_row):
        block = b1[group_rows(coarse_row), :]
        high = block.astype(BF16)
        low = (block - high.astype(F32)).astype(BF16)
        turned = high.T.astype(F32)
        fixed = turned[:64] + low.T[:64].astype(F32)
        for half in range(2):
            rows = [turned[32 * j + 16 * half : 32 * j + 16 * half + 16] for j in range(4)]
            own[half, pl.ds(coarse_row, PART, stride=OSTRIDE), :] = (
                fixed[16 * half : 16 * half + 16] + fixed[32 + 16 * half : 48 + 16 * half]
            )
            keep_off(4, half, coarse_row, rows[2])
            keep_off(5, half, coarse_row, rows[3])

    loop(BS, 4, finish_outer)

    def own_rows():
        return jnp.concatenate(
            [
                jnp.concatenate(
                    [own[half, pl.ds(c * OSTRIDE, BS), :] for c in range(PART)], axis=0
                )
                for half in range(2)
            ],
            axis=1,
        )

    high = own_rows().astype(BF16)
    pack(2, high)
    third = exchange(2)
    for copy in third:
        copy.start()

    def finish_local(coarse_row):
        turned = b0[group_rows(coarse_row), :].astype(BF16).T.astype(F32)
        for half in range(2):
            for j in range(4):
                keep_off(j, half, coarse_row, turned[32 * j + 16 * half : 32 * j + 16 * half + 16])

    loop(BS, 4, finish_local)

    whole = own_rows()
    high = whole.astype(BF16)
    low = (whole - high.astype(F32)).astype(BF16)
    total = whole + jnp.dot(high, plan_perm[...], preferred_element_type=F32)
    total = total + jnp.dot(low, plan_perm[...], preferred_element_type=F32)
    for copy in third:
        copy.wait()
    total = total + arrived(2)
    for half in range(2):
        xf[half, pl.ds(0, PART * BS), :] = total[:, half * LAYER : (half + 1) * LAYER]


def finish(p_ref, d_ref, low_ref, high_ref, p_out, d_out, o_out, planes, sems):
    early = [pltpu.make_async_copy(p_ref, p_out, sems.at[0])] + [
        pltpu.make_async_copy(
            d_ref.at[half, pl.ds(0, PART * BS)],
            d_out.at[:, pl.ds(half * LAYER, LAYER)],
            sems.at[1 + half],
        )
        for half in range(2)
    ]
    for copy in early:
        copy.start()
    late = []
    for chunk in range(4):

        def narrow(step):
            coarse = 4 * chunk + step
            for slot in range(6):
                for half, source in enumerate((low_ref, high_ref)):
                    rows = source[pl.ds(coarse * CSTRIDE + slot * BS, BS), :]
                    planes[coarse * 6 + slot, :, half * LAYER : (half + 1) * LAYER] = rows.astype(BF16)

        loop(4, 1, narrow)
        there = pl.ds(24 * chunk, 24)
        late.append(pltpu.make_async_copy(planes.at[there], o_out.at[there], sems.at[3 + chunk]))
        late[-1].start()
    for copy in (*early, *late):
        copy.wait()


def on_device(operator_blocks, tentative, jacobi_scale, columns):
    rows = columns.shape[1]
    vmem = pl.BlockSpec(memory_space=pltpu.VMEM)
    hbm = pl.BlockSpec(memory_space=pl.ANY)
    kept = pl.pallas_call(
        kernel,
        out_shape=(
            pltpu.VMEM((BS, PART, rows), BF16),
            pltpu.VMEM((2, BS * XSTRIDE, LAYER), F32),
            pltpu.VMEM((BS * STRIDE, 128), F32),
            pltpu.VMEM((BS * STRIDE, 128), F32),
        ),
        in_specs=[hbm, vmem, vmem, vmem],
        out_specs=(vmem,) * 4,
        scratch_shapes=[
            pltpu.VMEM((2, 2, BS, BS, rows), BF16),
            *[pltpu.VMEM((BS * STRIDE, 128), F32) for _ in range(5)],
            pltpu.VMEM((LAYER, BS, 128), BF16),
            pltpu.VMEM((BS * STRIDE, 128), F32),
            pltpu.VMEM((2, LAYER, 128, 128), BF16),
            pltpu.VMEM((BS, PART, rows), BF16),
            pltpu.VMEM((PART, BS, rows), BF16),
            pltpu.VMEM((3, PART, BS, rows), BF16),
            pltpu.VMEM((BS, PART, LAYER), BF16),
            pltpu.VMEM((BS, PART, LAYER), BF16),
            pltpu.VMEM((2, PART * OSTRIDE, LAYER), F32),
            pltpu.VMEM((2, BS, LAYER), F32),
            pltpu.VMEM((rows, rows), BF16),
            pltpu.VMEM((2 * PART, rows), BF16),
            pltpu.VMEM((2 * PART, rows), BF16),
            pltpu.VMEM((3, 2, PART, BS * PART), BF16),
            pltpu.VMEM((3, 2, PART, BS * PART), BF16),
            pltpu.SemaphoreType.DMA((2,)),
            pltpu.SemaphoreType.DMA((4,)),
            pltpu.SemaphoreType.DMA((14,)),
            pltpu.SemaphoreType.DMA((14,)),
        ],
        compiler_params=pltpu.CompilerParams(
            collective_id=0, has_side_effects=True, vmem_limit_bytes=51 * 2**20
        ),
    )(operator_blocks, tentative, jacobi_scale, columns)
    prolongator, diag, off = pl.pallas_call(
        finish,
        out_shape=(
            jax.ShapeDtypeStruct((BS, PART, rows), BF16),
            jax.ShapeDtypeStruct((PART * BS, rows), F32),
            jax.ShapeDtypeStruct((PART * 6, BS, rows), BF16),
        ),
        in_specs=[vmem] * 4,
        out_specs=(hbm,) * 3,
        scratch_shapes=[
            pltpu.VMEM((PART * 6, BS, rows), BF16),
            pltpu.SemaphoreType.DMA((7,)),
        ],
        compiler_params=pltpu.CompilerParams(vmem_limit_bytes=8 * 2**20),
    )(*kept)
    return prolongator, diag.reshape(PART, BS, rows), off.reshape(PART, 6, BS, rows)


def solution(mesh):
    placed = (
        P(None, None, None, "rows"),
        P(None, "cols", "rows"),
        P(None, "rows"),
        P(None, "rows"),
    )
    return jax.shard_map(
        on_device,
        mesh=mesh,
        in_specs=placed,
        out_specs=(P(None, "cols", "rows"), P("cols", None, "rows"), P("cols", None, None, "rows")),
        check_vma=False,
    )
```

```python
import functools

import jax
import jax.numpy as jnp
from jax import lax
from jax.experimental import pallas as pl
from jax.experimental.pallas import tpu as pltpu
from jax.sharding import PartitionSpec as P

GX = 8
GY = 16
LAYER = GX * GY
BS = 64
PART = 16
STRIDE = LAYER + 4
CSTRIDE = 388
OSTRIDE = BS + 4
XSTRIDE = PART + 4
BIG = 1 << 20
MESH = pl.DeviceIdType.MESH
F32 = jnp.float32
BF16 = jnp.bfloat16
NT = (((1,), (1,)), ((), ()))
TN = (((0,), (0,)), ((), ()))


def iota(shape, dim):
    return lax.broadcasted_iota(jnp.int32, shape, dim)


def group_rows(block):
    return pl.ds(block * STRIDE, LAYER)


def of_position(position):
    return pl.ds(position, BS, stride=STRIDE)


def loop(count, unroll, body):
    def step(index, carry):
        for inner in range(unroll):
            body(index * unroll + inner)
        return carry

    lax.fori_loop(0, count // unroll, step, 0)


def relay_one(stage, targets, fine):
    for half in range(2):
        block = stage[:, fine, :, half * LAYER : (half + 1) * LAYER].reshape(128, LAYER)
        targets[half][group_rows(fine), :] = block.T.astype(F32)


def relay(stage, targets):
    loop(BS, 8, lambda fine: relay_one(stage, targets, fine))


def spread(rows_of, target):
    def body(fine):
        target[group_rows(fine), :] = jnp.concatenate(rows_of(fine), axis=0).T.astype(F32)

    loop(BS, 16, body)


def halves(ref, index):
    return ref[index, :, :LAYER], ref[index, :, LAYER:]


def left_of(sources, position):
    return jnp.concatenate(
        [source[of_position(position), :] for source in sources], axis=0
    ).astype(BF16)


def pick_plan(columns, device, far, near):
    count = columns.shape[1]
    partner = columns[1:2, :]
    row = iota((1, count), 1).astype(F32)
    value = partner.astype(F32)
    perm = (iota((count, count), 0) == partner - device * count).astype(BF16)
    order = iota((PART, count), 0)
    send, take = [], []
    for other in (far, near):
        there = (partner >= other * count) & (partner < (other + 1) * count)
        for entry, found in ((row, send), (value, take)):
            first = jnp.min(jnp.where(there, entry, float(BIG)), axis=1, keepdims=True)
            last = jnp.max(jnp.where(there, entry, -1.0), axis=1, keepdims=True)
            wanted = jnp.where(order == 0, first, jnp.where(order == 1, last, -2.0))
            hit = jnp.where(there, entry, -3.0) == wanted
            found.append(hit.astype(F32).astype(BF16))
    return perm, jnp.concatenate(send, axis=0), jnp.concatenate(take, axis=0)


def kernel(
    a_hbm, t_ref, s_ref, col_ref, pxl, xf, b2, b3,
    stage, b0, b1, b4, b5, b6, pn, yx, rr, other, pc, gath, below, above, own, s32, plan_perm, plan_send,
    plan_take, snd, rcv, in_sem, chunk_sem, send_sem, recv_sem,
):
    device = lax.axis_index("rows")
    part = lax.axis_index("cols")
    devices = lax.axis_size("rows")
    parts = lax.axis_size("cols")
    far = lax.rem(device + devices // 2, devices)
    near = device + 1 - 2 * lax.rem(device, 2)
    up = lax.rem(device + 1, devices)
    down = lax.rem(device + devices - 1, devices)
    right = lax.rem(part + 1, parts)
    left = lax.rem(part + parts - 1, parts)
    opposite = lax.rem(part + 2, parts)

    def fetch(pair, slot):
        return pltpu.make_async_copy(a_hbm.at[pl.ds(2 * pair, 2)], stage.at[slot], in_sem.at[slot])

    def send(source, target, index, to):
        return pltpu.make_async_remote_copy(
            src_ref=source, dst_ref=target, send_sem=send_sem.at[index],
            recv_sem=recv_sem.at[index], device_id=to, device_id_type=MESH,
        )

    def exchange(turn):
        return [
            send(snd.at[turn, kind], rcv.at[turn, kind], 2 * turn + kind, (who, part))
            for kind, who in ((0, far), (1, near))
        ]

    def first_fetch(chunk):
        rows = pl.ds(chunk * 16, 16)
        return pltpu.make_async_copy(
            a_hbm.at[pl.ds(0, 2), rows], stage.at[0, :, rows], chunk_sem.at[chunk]
        )

    for chunk in range(4):
        first_fetch(chunk).start()
    fetch(1, 1).start()
    barrier = pltpu.get_barrier_semaphore()
    for who in ((far, part), (up, part), (down, part), (device, right), (device, left)):
        pl.semaphore_signal(barrier, inc=1, device_id=who, device_id_type=MESH)

    perm, send_rows, take_rows = pick_plan(col_ref, device, far, near)
    plan_perm[...] = perm
    plan_send[...] = send_rows
    plan_take[...] = take_rows
    for half in range(2):
        s32[half] = s_ref[:, half * LAYER : (half + 1) * LAYER].astype(F32)

    def pack(turn, matrix):
        rows = lax.dot_general(plan_send[...], matrix, NT, preferred_element_type=F32).astype(BF16)
        snd[turn, 0] = rows[:PART]
        snd[turn, 1] = rows[PART:]

    def arrived(turn):
        rows = rcv[turn].reshape(2 * PART, -1)
        return lax.dot_general(rows, plan_take[...], TN, preferred_element_type=F32)

    pack(0, t_ref[...].reshape(BS * PART, 2 * LAYER))
    pl.semaphore_wait(barrier, 5)
    first = exchange(0)
    for copy in first:
        copy.start()

    for chunk in range(4):
        first_fetch(chunk).wait()
        loop(16, 8, lambda fine: relay_one(stage.at[0], (b0, b1), 16 * chunk + fine))
    fetch(2, 0).start()

    fetch(1, 1).wait()
    relay(stage.at[1], (b2, b3))
    fetch(3, 1).start()
    for copy in first:
        copy.wait()
    moved = jnp.dot(
        t_ref[...].reshape(BS * PART, 2 * LAYER), plan_perm[...], preferred_element_type=F32
    )
    other[...] = (moved + arrived(0)).astype(BF16).reshape(BS, PART, 2 * LAYER)

    tt, cp = yx, b6
    spread(lambda fine: [*halves(t_ref, fine), *halves(other, fine)] * 2, tt)

    lane = iota((1, 128), 1)
    mask = [((lane >= 32 * j) & (lane < 32 * j + 32)).astype(F32).astype(BF16) for j in range(4)]
    own_low = ((lane & 63) < 32).astype(F32).astype(BF16)
    own_high = ((lane & 63) >= 32).astype(F32).astype(BF16)
    first_layer = (iota((BS, 128), 1) & 16) == 0
    keep = ((iota((128, 128), 1) & 16) == 0) == (iota((128, 128), 0) < BS)

    def smooth(position):
        block = tt[of_position(position), :].astype(BF16)
        right_side = jnp.concatenate([block * own_low, block * own_high], axis=0)
        result = jnp.dot(left_of((b0, b1), position), right_side, preferred_element_type=F32)
        cp[of_position(position), :] = jnp.where(first_layer, result[:BS], result[BS:])

    loop(LAYER, 32, smooth)

    def back(pair):
        fine = 2 * pair
        joined = jnp.where(
            iota((LAYER, 128), 1) < 64, cp[group_rows(fine), :], cp[group_rows(fine + 1), :]
        ).T
        for step in range(2):
            for half in range(2):
                base = 64 * step + 16 * half
                coupled = joined[base : base + 16] + joined[base + 32 : base + 48]
                lanes = pl.ds(half * LAYER, LAYER)
                value = t_ref[fine + step, :, lanes].astype(F32)
                value = value - s32[half, pl.ds(fine + step, 1), :] * coupled
                value = value.astype(BF16)
                pxl[fine + step, :, lanes] = value
                rows = pl.ds((fine + step) * XSTRIDE, PART)
                xf[half, rows, :] = value.astype(F32)

    loop(BS // 2, 4, back)

    def swap(coarse):
        for half in range(2):
            rows = xf[half, pl.ds(coarse, BS, stride=XSTRIDE), :]
            pc[coarse, :, half * LAYER : (half + 1) * LAYER] = rows.astype(BF16)

    loop(PART, 4, swap)
    pack(1, pxl[...].reshape(BS * PART, 2 * LAYER))

    middle = PART // 2
    low = pl.ds(0, middle)
    high = pl.ds(middle, middle)
    first_half = [
        send(pc.at[low], gath.at[0, low], 6, (device, right)),
        send(pc.at[high], gath.at[1, high], 7, (device, left)),
    ]
    second_half = [
        send(pc.at[high], gath.at[0, high], 12, (device, right)),
        send(pc.at[low], gath.at[1, low], 13, (device, left)),
    ]
    relays = [
        send(gath.at[0, low], gath.at[2, low], 10, (device, right)),
        send(gath.at[1, high], gath.at[2, high], 11, (device, left)),
    ]
    halo = [
        send(pxl.at[:, :, pl.ds(LAYER, LAYER)], below, 8, (up, part)),
        send(pxl.at[:, :, pl.ds(0, LAYER)], above, 9, (down, part)),
    ]
    second = exchange(1)
    for copy in (*second, *first_half, *halo, *second_half):
        copy.start()

    spread(lambda fine: [*halves(pxl, fine)] * 4, yx)

    def settle(position):
        pn[position] = yx[of_position(position), :].astype(BF16)

    loop(LAYER, 8, settle)
    fetch(2, 0).wait()
    relay(stage.at[0], (b4, b5))
    for copy in first_half:
        copy.wait_recv()
    for copy in relays:
        copy.start()
    fetch(3, 1).wait()

    def reach(slot, pairs, blocks, position):
        left_side = jnp.concatenate([left_of(pair, position) for pair in pairs], axis=1)
        right_side = jnp.concatenate([block * m for block, m in zip(blocks, mask)], axis=0)
        result = jnp.dot(left_side, right_side, preferred_element_type=F32)
        rr[slot, position] = jnp.where(keep, result, 0.0).astype(BF16)

    def local_line(line, carry):
        before = lax.rem(line + GY - 1, GY) * GX
        after = lax.rem(line + 1, GY) * GX
        base = line * GX
        for x in range(GX):
            blocks = [
                pn[base + (x + GX - 1) % GX], pn[base + (x + 1) % GX], pn[before + x], pn[after + x]
            ]
            reach(0, ((b2, b3), (b4, b5)), blocks, base + x)
        for inner in range(4):
            relay_one(stage.at[1], (b6, yx), line * 4 + inner)
        return carry

    def two_lines(index, carry):
        return local_line(2 * index + 1, local_line(2 * index, carry))

    lax.fori_loop(0, GY // 2, two_lines, 0)

    for copy in second:
        copy.wait()
    moved = jnp.dot(
        pxl[...].reshape(BS * PART, 2 * LAYER), plan_perm[...], preferred_element_type=F32
    )
    other[...] = (moved + arrived(1)).astype(BF16).reshape(BS, PART, 2 * LAYER)
    for copy in halo:
        copy.wait()

    def outer_rows(fine):
        low, high = halves(pxl, fine)
        return [low, high, *halves(other, fine), below[fine], low, high, above[fine]]

    spread(outer_rows, b2)

    def remote_row(position):
        block = b2[of_position(position), :].astype(BF16)
        reach(1, ((b0, b1), (b6, yx)), [block] * 4, position)

    loop(LAYER, 32, remote_row)

    pf, off = b4, (b2, b3)

    def wide(source, index, place):
        def body(coarse):
            block = source[coarse] if index is None else source[index, coarse]
            rows = jnp.concatenate([block[:, :LAYER], block[:, LAYER:]], axis=0)
            pf[group_rows(place * PART + coarse), :] = rows.T.astype(F32)

        loop(PART, 16, body)

    def product(slots, start, count):
        def body(position):
            rows = pl.ds(start * STRIDE + position, count, stride=STRIDE)
            left_side = pf[rows, :].astype(BF16)
            right_side = [rr[slot, position] for slot in slots]
            right_side = right_side[0] if len(slots) == 1 else jnp.concatenate(right_side, axis=1)
            result = jnp.dot(left_side, right_side, preferred_element_type=F32)
            for order, slot in enumerate(slots):
                (b0, b1)[slot][rows, :] = result[:, order * 128 : (order + 1) * 128]

        loop(LAYER, 32, body)

    owners = (part, left, right, opposite)

    def keep_off(slot, half, coarse_row, rows):
        start = slot * BS + coarse_row
        off[half][pl.ds(start, PART, stride=CSTRIDE), :] = rows

    def finish_outer(place):
        def body(coarse):
            block = b1[group_rows(place * PART + coarse), :]
            coarse_row = owners[place] * PART + coarse
            high = block.astype(BF16)
            low = (block - high.astype(F32)).astype(BF16)
            turned = high.T.astype(F32)
            fixed = turned[:64] + low.T[:64].astype(F32)
            for half in range(2):
                base = 16 * half
                own[half, pl.ds(coarse_row, PART, stride=OSTRIDE), :] = (
                    fixed[base : base + 16] + fixed[base + 32 : base + 48]
                )
                keep_off(4, half, coarse_row, turned[base + 64 : base + 80])
                keep_off(5, half, coarse_row, turned[base + 96 : base + 112])

        loop(PART, 16, body)

    wide(pc, None, 0)
    for copy in first_half:
        copy.wait_send()
    for copy in second_half:
        copy.wait()
    wide(gath, 0, 1)
    wide(gath, 1, 2)
    product((0, 1), 0, 3 * PART)
    for place in range(3):
        finish_outer(place)
    for copy in relays:
        copy.wait()
    wide(gath, 2, 3)
    product((1,), 3 * PART, PART)
    finish_outer(3)

    def own_rows():
        return jnp.concatenate(
            [
                jnp.concatenate(
                    [own[half, pl.ds(c * OSTRIDE, BS), :] for c in range(PART)], axis=0
                )
                for half in range(2)
            ],
            axis=1,
        )

    high = own_rows().astype(BF16)
    pack(2, high)
    third = exchange(2)
    for copy in third:
        copy.start()

    product((0,), 3 * PART, PART)

    def finish_local(place):
        def body(coarse):
            turned = b0[group_rows(place * PART + coarse), :].astype(BF16).T.astype(F32)
            coarse_row = owners[place] * PART + coarse
            for half in range(2):
                for j in range(4):
                    base = 32 * j + 16 * half
                    keep_off(j, half, coarse_row, turned[base : base + 16])

        loop(PART, 16, body)

    for place in range(4):
        finish_local(place)
    whole = own_rows()
    high = whole.astype(BF16)
    low = (whole - high.astype(F32)).astype(BF16)
    total = whole + jnp.dot(high, plan_perm[...], preferred_element_type=F32)
    total = total + jnp.dot(low, plan_perm[...], preferred_element_type=F32)
    for copy in third:
        copy.wait()
    total = total + arrived(2)
    for half in range(2):
        xf[half, pl.ds(0, PART * BS), :] = total[:, half * LAYER : (half + 1) * LAYER]


def finish(p_ref, d_ref, low_ref, high_ref, p_out, d_out, o_out, planes, sems):
    early = [pltpu.make_async_copy(p_ref, p_out, sems.at[0])] + [
        pltpu.make_async_copy(
            d_ref.at[half, pl.ds(0, PART * BS)],
            d_out.at[:, pl.ds(half * LAYER, LAYER)],
            sems.at[1 + half],
        )
        for half in range(2)
    ]
    for copy in early:
        copy.start()
    late = []
    for chunk in range(4):

        def narrow(step):
            coarse = 4 * chunk + step
            for slot in range(6):
                for half, source in enumerate((low_ref, high_ref)):
                    rows = source[pl.ds(coarse * CSTRIDE + slot * BS, BS), :]
                    planes[coarse * 6 + slot, :, half * LAYER : (half + 1) * LAYER] = rows.astype(BF16)

        loop(4, 1, narrow)
        there = pl.ds(24 * chunk, 24)
        late.append(pltpu.make_async_copy(planes.at[there], o_out.at[there], sems.at[3 + chunk]))
        late[-1].start()
    for copy in (*early, *late):
        copy.wait()


def on_device(operator_blocks, tentative, jacobi_scale, columns):
    rows = columns.shape[1]
    vmem = pl.BlockSpec(memory_space=pltpu.VMEM)
    hbm = pl.BlockSpec(memory_space=pl.ANY)
    kept = pl.pallas_call(
        kernel,
        out_shape=(
            pltpu.VMEM((BS, PART, rows), BF16),
            pltpu.VMEM((2, BS * XSTRIDE, LAYER), F32),
            pltpu.VMEM((BS * STRIDE, 128), F32),
            pltpu.VMEM((BS * STRIDE, 128), F32),
        ),
        in_specs=[hbm, vmem, vmem, vmem],
        out_specs=(vmem,) * 4,
        scratch_shapes=[
            pltpu.VMEM((2, 2, BS, BS, rows), BF16),
            *[pltpu.VMEM((BS * STRIDE, 128), F32) for _ in range(5)],
            pltpu.VMEM((LAYER, BS, 128), BF16),
            pltpu.VMEM((BS * STRIDE, 128), F32),
            pltpu.VMEM((2, LAYER, 128, 128), BF16),
            pltpu.VMEM((BS, PART, rows), BF16),
            pltpu.VMEM((PART, BS, rows), BF16),
            pltpu.VMEM((3, PART, BS, rows), BF16),
            pltpu.VMEM((BS, PART, LAYER), BF16),
            pltpu.VMEM((BS, PART, LAYER), BF16),
            pltpu.VMEM((2, PART * OSTRIDE, LAYER), F32),
            pltpu.VMEM((2, BS, LAYER), F32),
            pltpu.VMEM((rows, rows), BF16),
            pltpu.VMEM((2 * PART, rows), BF16),
            pltpu.VMEM((2 * PART, rows), BF16),
            pltpu.VMEM((3, 2, PART, BS * PART), BF16),
            pltpu.VMEM((3, 2, PART, BS * PART), BF16),
            pltpu.SemaphoreType.DMA((2,)),
            pltpu.SemaphoreType.DMA((4,)),
            pltpu.SemaphoreType.DMA((14,)),
            pltpu.SemaphoreType.DMA((14,)),
        ],
        compiler_params=pltpu.CompilerParams(
            collective_id=0, has_side_effects=True, vmem_limit_bytes=51 * 2**20
        ),
    )(operator_blocks, tentative, jacobi_scale, columns)
    prolongator, diag, off = pl.pallas_call(
        finish,
        out_shape=(
            jax.ShapeDtypeStruct((BS, PART, rows), BF16),
            jax.ShapeDtypeStruct((PART * BS, rows), F32),
            jax.ShapeDtypeStruct((PART * 6, BS, rows), BF16),
        ),
        in_specs=[vmem] * 4,
        out_specs=(hbm,) * 3,
        scratch_shapes=[
            pltpu.VMEM((PART * 6, BS, rows), BF16),
            pltpu.SemaphoreType.DMA((7,)),
        ],
        compiler_params=pltpu.CompilerParams(vmem_limit_bytes=8 * 2**20),
    )(*kept)
    return prolongator, diag.reshape(PART, BS, rows), off.reshape(PART, 6, BS, rows)


def solution(mesh):
    placed = (
        P(None, None, None, "rows"),
        P(None, "cols", "rows"),
        P(None, "rows"),
        P(None, "rows"),
    )
    return jax.shard_map(
        on_device,
        mesh=mesh,
        in_specs=placed,
        out_specs=(P(None, "cols", "rows"), P("cols", None, "rows"), P("cols", None, None, "rows")),
        check_vma=False,
    )
```

```python
import functools

import jax
import jax.numpy as jnp
from jax import lax
from jax.experimental import pallas as pl
from jax.experimental.pallas import tpu as pltpu
from jax.sharding import PartitionSpec as P

GX = 8
GY = 16
LAYER = GX * GY
BS = 64
PART = 16
STRIDE = LAYER + 4
CSTRIDE = 388
OSTRIDE = BS + 4
XSTRIDE = PART + 4
BIG = 1 << 20
MESH = pl.DeviceIdType.MESH
F32 = jnp.float32
BF16 = jnp.bfloat16
NT = (((1,), (1,)), ((), ()))
TN = (((0,), (0,)), ((), ()))


def iota(shape, dim):
    return lax.broadcasted_iota(jnp.int32, shape, dim)


def group_rows(block):
    return pl.ds(block * STRIDE, LAYER)


def of_position(position):
    return pl.ds(position, BS, stride=STRIDE)


def loop(count, unroll, body):
    def step(index, carry):
        for inner in range(unroll):
            body(index * unroll + inner)
        return carry

    lax.fori_loop(0, count // unroll, step, 0)


def relay_one(stage, targets, fine):
    for half in range(2):
        block = stage[:, fine, :, half * LAYER : (half + 1) * LAYER].reshape(128, LAYER)
        targets[half][group_rows(fine), :] = block.T.astype(F32)


def relay(stage, targets):
    loop(BS, 8, lambda fine: relay_one(stage, targets, fine))


def spread(rows_of, target):
    def body(fine):
        target[group_rows(fine), :] = jnp.concatenate(rows_of(fine), axis=0).T.astype(F32)

    loop(BS, 16, body)


def halves(ref, index):
    return ref[index, :, :LAYER], ref[index, :, LAYER:]


def left_of(sources, position):
    return jnp.concatenate(
        [source[of_position(position), :] for source in sources], axis=0
    ).astype(BF16)


def pick_plan(columns, device, far, near):
    count = columns.shape[1]
    partner = columns[1:2, :]
    row = iota((1, count), 1).astype(F32)
    value = partner.astype(F32)
    perm = (iota((count, count), 0) == partner - device * count).astype(BF16)
    order = iota((PART, count), 0)
    send, take = [], []
    for other in (far, near):
        there = (partner >= other * count) & (partner < (other + 1) * count)
        for entry, found in ((row, send), (value, take)):
            first = jnp.min(jnp.where(there, entry, float(BIG)), axis=1, keepdims=True)
            last = jnp.max(jnp.where(there, entry, -1.0), axis=1, keepdims=True)
            wanted = jnp.where(order == 0, first, jnp.where(order == 1, last, -2.0))
            hit = jnp.where(there, entry, -3.0) == wanted
            found.append(hit.astype(F32).astype(BF16))
    return perm, jnp.concatenate(send, axis=0), jnp.concatenate(take, axis=0)


def kernel(
    a_hbm, t_ref, s_ref, col_ref, pxl, xf, b2, b3,
    stage, b0, b1, b4, b5, b6, pn, yx, rr, other, pc, gath, below, above, own, s32, plan_perm, plan_send,
    plan_take, snd, rcv, in_sem, chunk_sem, send_sem, recv_sem,
):
    device = lax.axis_index("rows")
    part = lax.axis_index("cols")
    devices = lax.axis_size("rows")
    parts = lax.axis_size("cols")
    far = lax.rem(device + devices // 2, devices)
    near = device + 1 - 2 * lax.rem(device, 2)
    up = lax.rem(device + 1, devices)
    down = lax.rem(device + devices - 1, devices)
    right = lax.rem(part + 1, parts)
    left = lax.rem(part + parts - 1, parts)
    opposite = lax.rem(part + 2, parts)

    def fetch(pair, slot):
        return pltpu.make_async_copy(a_hbm.at[pl.ds(2 * pair, 2)], stage.at[slot], in_sem.at[slot])

    def send(source, target, index, to):
        return pltpu.make_async_remote_copy(
            src_ref=source, dst_ref=target, send_sem=send_sem.at[index],
            recv_sem=recv_sem.at[index], device_id=to, device_id_type=MESH,
        )

    def exchange(turn):
        return [
            send(snd.at[turn, kind], rcv.at[turn, kind], 2 * turn + kind, (who, part))
            for kind, who in ((0, far), (1, near))
        ]

    def first_fetch(chunk):
        rows = pl.ds(chunk * 16, 16)
        return pltpu.make_async_copy(
            a_hbm.at[pl.ds(0, 2), rows], stage.at[0, :, rows], chunk_sem.at[chunk]
        )

    for chunk in range(4):
        first_fetch(chunk).start()
    fetch(1, 1).start()
    barrier = pltpu.get_barrier_semaphore()
    for who in ((far, part), (up, part), (down, part), (device, right), (device, left)):
        pl.semaphore_signal(barrier, inc=1, device_id=who, device_id_type=MESH)

    perm, send_rows, take_rows = pick_plan(col_ref, device, far, near)
    plan_perm[...] = perm
    plan_send[...] = send_rows
    plan_take[...] = take_rows
    for half in range(2):
        s32[half] = s_ref[:, half * LAYER : (half + 1) * LAYER].astype(F32)

    def pack(turn, matrix):
        rows = lax.dot_general(plan_send[...], matrix, NT, preferred_element_type=F32).astype(BF16)
        snd[turn, 0] = rows[:PART]
        snd[turn, 1] = rows[PART:]

    def arrived(turn):
        rows = rcv[turn].reshape(2 * PART, -1)
        return lax.dot_general(rows, plan_take[...], TN, preferred_element_type=F32)

    pack(0, t_ref[...].reshape(BS * PART, 2 * LAYER))
    pl.semaphore_wait(barrier, 5)
    first = exchange(0)
    for copy in first:
        copy.start()

    for chunk in range(4):
        first_fetch(chunk).wait()
        loop(16, 8, lambda fine: relay_one(stage.at[0], (b0, b1), 16 * chunk + fine))
    fetch(2, 0).start()

    fetch(1, 1).wait()
    relay(stage.at[1], (b2, b3))
    fetch(3, 1).start()
    for copy in first:
        copy.wait()
    moved = jnp.dot(
        t_ref[...].reshape(BS * PART, 2 * LAYER), plan_perm[...], preferred_element_type=F32
    )
    other[...] = (moved + arrived(0)).astype(BF16).reshape(BS, PART, 2 * LAYER)

    tt, cp = yx, b6
    spread(lambda fine: [*halves(t_ref, fine), *halves(other, fine)] * 2, tt)

    lane = iota((1, 128), 1)
    mask = [((lane >= 32 * j) & (lane < 32 * j + 32)).astype(F32).astype(BF16) for j in range(4)]
    own_low = ((lane & 63) < 32).astype(F32).astype(BF16)
    own_high = ((lane & 63) >= 32).astype(F32).astype(BF16)
    first_layer = (iota((BS, 128), 1) & 16) == 0
    keep = ((iota((128, 128), 1) & 16) == 0) == (iota((128, 128), 0) < BS)

    def smooth(position):
        block = tt[of_position(position), :].astype(BF16)
        right_side = jnp.concatenate([block * own_low, block * own_high], axis=0)
        result = jnp.dot(left_of((b0, b1), position), right_side, preferred_element_type=F32)
        cp[of_position(position), :] = jnp.where(first_layer, result[:BS], result[BS:])

    loop(LAYER, 32, smooth)

    def back(pair):
        fine = 2 * pair
        joined = jnp.where(
            iota((LAYER, 128), 1) < 64, cp[group_rows(fine), :], cp[group_rows(fine + 1), :]
        ).T
        for step in range(2):
            for half in range(2):
                base = 64 * step + 16 * half
                coupled = joined[base : base + 16] + joined[base + 32 : base + 48]
                lanes = pl.ds(half * LAYER, LAYER)
                value = t_ref[fine + step, :, lanes].astype(F32)
                value = value - s32[half, pl.ds(fine + step, 1), :] * coupled
                value = value.astype(BF16)
                pxl[fine + step, :, lanes] = value
                rows = pl.ds((fine + step) * XSTRIDE, PART)
                xf[half, rows, :] = value.astype(F32)

    loop(BS // 2, 4, back)

    def swap(coarse):
        for half in range(2):
            rows = xf[half, pl.ds(coarse, BS, stride=XSTRIDE), :]
            pc[coarse, :, half * LAYER : (half + 1) * LAYER] = rows.astype(BF16)

    loop(PART, 4, swap)
    pack(1, pxl[...].reshape(BS * PART, 2 * LAYER))

    middle = PART // 2
    low = pl.ds(0, middle)
    high = pl.ds(middle, middle)
    first_half = [
        send(pc.at[low], gath.at[0, low], 6, (device, right)),
        send(pc.at[high], gath.at[1, high], 7, (device, left)),
    ]
    second_half = [
        send(pc.at[high], gath.at[0, high], 12, (device, right)),
        send(pc.at[low], gath.at[1, low], 13, (device, left)),
    ]
    relays = [
        send(gath.at[0, low], gath.at[2, low], 10, (device, right)),
        send(gath.at[1, high], gath.at[2, high], 11, (device, left)),
    ]
    halo = [
        send(pxl.at[:, :, pl.ds(LAYER, LAYER)], below, 8, (up, part)),
        send(pxl.at[:, :, pl.ds(0, LAYER)], above, 9, (down, part)),
    ]
    second = exchange(1)
    for copy in (*first_half, *second_half, *second, *halo):
        copy.start()

    spread(lambda fine: [*halves(pxl, fine)] * 4, yx)

    def settle(position):
        pn[position] = yx[of_position(position), :].astype(BF16)

    loop(LAYER, 8, settle)
    fetch(2, 0).wait()
    relay(stage.at[0], (b4, b5))
    fetch(3, 1).wait()

    def reach(slot, pairs, blocks, position):
        left_side = jnp.concatenate([left_of(pair, position) for pair in pairs], axis=1)
        right_side = jnp.concatenate([block * m for block, m in zip(blocks, mask)], axis=0)
        result = jnp.dot(left_side, right_side, preferred_element_type=F32)
        rr[slot, position] = jnp.where(keep, result, 0.0).astype(BF16)

    def local_line(line, carry):
        before = lax.rem(line + GY - 1, GY) * GX
        after = lax.rem(line + 1, GY) * GX
        base = line * GX
        for x in range(GX):
            blocks = [
                pn[base + (x + GX - 1) % GX], pn[base + (x + 1) % GX], pn[before + x], pn[after + x]
            ]
            reach(0, ((b2, b3), (b4, b5)), blocks, base + x)
        for inner in range(4):
            relay_one(stage.at[1], (b6, yx), line * 4 + inner)
        return carry

    def two_lines(index, carry):
        return local_line(2 * index + 1, local_line(2 * index, carry))

    lax.fori_loop(0, GY // 2, two_lines, 0)

    for copy in second:
        copy.wait()
    moved = jnp.dot(
        pxl[...].reshape(BS * PART, 2 * LAYER), plan_perm[...], preferred_element_type=F32
    )
    other[...] = (moved + arrived(1)).astype(BF16).reshape(BS, PART, 2 * LAYER)
    for copy in halo:
        copy.wait()

    def outer_rows(fine):
        low, high = halves(pxl, fine)
        return [low, high, *halves(other, fine), below[fine], low, high, above[fine]]

    spread(outer_rows, b2)
    for copy in first_half:
        copy.wait_recv()
    for copy in relays:
        copy.start()

    def remote_row(position):
        block = b2[of_position(position), :].astype(BF16)
        reach(1, ((b0, b1), (b6, yx)), [block] * 4, position)

    loop(LAYER, 32, remote_row)

    pf, off = b4, (b2, b3)

    def wide(source, index, place):
        def body(coarse):
            block = source[coarse] if index is None else source[index, coarse]
            rows = jnp.concatenate([block[:, :LAYER], block[:, LAYER:]], axis=0)
            pf[group_rows(place * PART + coarse), :] = rows.T.astype(F32)

        loop(PART, 16, body)

    def product(slots, start, count):
        def body(position):
            rows = pl.ds(start * STRIDE + position, count, stride=STRIDE)
            left_side = pf[rows, :].astype(BF16)
            right_side = [rr[slot, position] for slot in slots]
            right_side = right_side[0] if len(slots) == 1 else jnp.concatenate(right_side, axis=1)
            result = jnp.dot(left_side, right_side, preferred_element_type=F32)
            for order, slot in enumerate(slots):
                (b0, b1)[slot][rows, :] = result[:, order * 128 : (order + 1) * 128]

        loop(LAYER, 32, body)

    owners = (part, left, right, opposite)

    def keep_off(slot, half, coarse_row, rows):
        start = slot * BS + coarse_row
        off[half][pl.ds(start, PART, stride=CSTRIDE), :] = rows

    def finish_outer(place):
        def body(coarse):
            block = b1[group_rows(place * PART + coarse), :]
            coarse_row = owners[place] * PART + coarse
            high = block.astype(BF16)
            low = (block - high.astype(F32)).astype(BF16)
            turned = high.T.astype(F32)
            fixed = turned[:64] + low.T[:64].astype(F32)
            for half in range(2):
                base = 16 * half
                own[half, pl.ds(coarse_row, PART, stride=OSTRIDE), :] = (
                    fixed[base : base + 16] + fixed[base + 32 : base + 48]
                )
                keep_off(4, half, coarse_row, turned[base + 64 : base + 80])
                keep_off(5, half, coarse_row, turned[base + 96 : base + 112])

        loop(PART, 16, body)

    wide(pc, None, 0)
    for copy in first_half:
        copy.wait_send()
    for copy in second_half:
        copy.wait()
    wide(gath, 0, 1)
    wide(gath, 1, 2)
    product((0, 1), 0, 3 * PART)
    for place in range(3):
        finish_outer(place)
    for copy in relays:
        copy.wait()
    wide(gath, 2, 3)
    product((1,), 3 * PART, PART)
    finish_outer(3)

    def own_rows():
        return jnp.concatenate(
            [
                jnp.concatenate(
                    [own[half, pl.ds(c * OSTRIDE, BS), :] for c in range(PART)], axis=0
                )
                for half in range(2)
            ],
            axis=1,
        )

    high = own_rows().astype(BF16)
    pack(2, high)
    third = exchange(2)
    for copy in third:
        copy.start()

    product((0,), 3 * PART, PART)

    def finish_local(place):
        def body(coarse):
            turned = b0[group_rows(place * PART + coarse), :].astype(BF16).T.astype(F32)
            coarse_row = owners[place] * PART + coarse
            for half in range(2):
                for j in range(4):
                    base = 32 * j + 16 * half
                    keep_off(j, half, coarse_row, turned[base : base + 16])

        loop(PART, 16, body)

    for place in range(4):
        finish_local(place)
    whole = own_rows()
    high = whole.astype(BF16)
    low = (whole - high.astype(F32)).astype(BF16)
    total = whole + jnp.dot(high, plan_perm[...], preferred_element_type=F32)
    total = total + jnp.dot(low, plan_perm[...], preferred_element_type=F32)
    for copy in third:
        copy.wait()
    total = total + arrived(2)
    for half in range(2):
        xf[half, pl.ds(0, PART * BS), :] = total[:, half * LAYER : (half + 1) * LAYER]


def finish(p_ref, d_ref, low_ref, high_ref, p_out, d_out, o_out, planes, sems):
    early = [pltpu.make_async_copy(p_ref, p_out, sems.at[0])] + [
        pltpu.make_async_copy(
            d_ref.at[half, pl.ds(0, PART * BS)],
            d_out.at[:, pl.ds(half * LAYER, LAYER)],
            sems.at[1 + half],
        )
        for half in range(2)
    ]
    for copy in early:
        copy.start()
    late = []
    for chunk in range(4):

        def narrow(step):
            coarse = 4 * chunk + step
            for slot in range(6):
                for half, source in enumerate((low_ref, high_ref)):
                    rows = source[pl.ds(coarse * CSTRIDE + slot * BS, BS), :]
                    planes[coarse * 6 + slot, :, half * LAYER : (half + 1) * LAYER] = rows.astype(BF16)

        loop(4, 1, narrow)
        there = pl.ds(24 * chunk, 24)
        late.append(pltpu.make_async_copy(planes.at[there], o_out.at[there], sems.at[3 + chunk]))
        late[-1].start()
    for copy in (*early, *late):
        copy.wait()


def on_device(operator_blocks, tentative, jacobi_scale, columns):
    rows = columns.shape[1]
    vmem = pl.BlockSpec(memory_space=pltpu.VMEM)
    hbm = pl.BlockSpec(memory_space=pl.ANY)
    kept = pl.pallas_call(
        kernel,
        out_shape=(
            pltpu.VMEM((BS, PART, rows), BF16),
            pltpu.VMEM((2, BS * XSTRIDE, LAYER), F32),
            pltpu.VMEM((BS * STRIDE, 128), F32),
            pltpu.VMEM((BS * STRIDE, 128), F32),
        ),
        in_specs=[hbm, vmem, vmem, vmem],
        out_specs=(vmem,) * 4,
        scratch_shapes=[
            pltpu.VMEM((2, 2, BS, BS, rows), BF16),
            *[pltpu.VMEM((BS * STRIDE, 128), F32) for _ in range(5)],
            pltpu.VMEM((LAYER, BS, 128), BF16),
            pltpu.VMEM((BS * STRIDE, 128), F32),
            pltpu.VMEM((2, LAYER, 128, 128), BF16),
            pltpu.VMEM((BS, PART, rows), BF16),
            pltpu.VMEM((PART, BS, rows), BF16),
            pltpu.VMEM((3, PART, BS, rows), BF16),
            pltpu.VMEM((BS, PART, LAYER), BF16),
            pltpu.VMEM((BS, PART, LAYER), BF16),
            pltpu.VMEM((2, PART * OSTRIDE, LAYER), F32),
            pltpu.VMEM((2, BS, LAYER), F32),
            pltpu.VMEM((rows, rows), BF16),
            pltpu.VMEM((2 * PART, rows), BF16),
            pltpu.VMEM((2 * PART, rows), BF16),
            pltpu.VMEM((3, 2, PART, BS * PART), BF16),
            pltpu.VMEM((3, 2, PART, BS * PART), BF16),
            pltpu.SemaphoreType.DMA((2,)),
            pltpu.SemaphoreType.DMA((4,)),
            pltpu.SemaphoreType.DMA((14,)),
            pltpu.SemaphoreType.DMA((14,)),
        ],
        compiler_params=pltpu.CompilerParams(
            collective_id=0, has_side_effects=True, vmem_limit_bytes=51 * 2**20
        ),
    )(operator_blocks, tentative, jacobi_scale, columns)
    prolongator, diag, off = pl.pallas_call(
        finish,
        out_shape=(
            jax.ShapeDtypeStruct((BS, PART, rows), BF16),
            jax.ShapeDtypeStruct((PART * BS, rows), F32),
            jax.ShapeDtypeStruct((PART * 6, BS, rows), BF16),
        ),
        in_specs=[vmem] * 4,
        out_specs=(hbm,) * 3,
        scratch_shapes=[
            pltpu.VMEM((PART * 6, BS, rows), BF16),
            pltpu.SemaphoreType.DMA((7,)),
        ],
        compiler_params=pltpu.CompilerParams(vmem_limit_bytes=8 * 2**20),
    )(*kept)
    return prolongator, diag.reshape(PART, BS, rows), off.reshape(PART, 6, BS, rows)


def solution(mesh):
    placed = (
        P(None, None, None, "rows"),
        P(None, "cols", "rows"),
        P(None, "rows"),
        P(None, "rows"),
    )
    return jax.shard_map(
        on_device,
        mesh=mesh,
        in_specs=placed,
        out_specs=(P(None, "cols", "rows"), P("cols", None, "rows"), P("cols", None, None, "rows")),
        check_vma=False,
    )
```

```python
import functools

import jax
import jax.numpy as jnp
from jax import lax
from jax.experimental import pallas as pl
from jax.experimental.pallas import tpu as pltpu
from jax.sharding import PartitionSpec as P

GX = 8
GY = 16
LAYER = GX * GY
BS = 64
PART = 16
STRIDE = LAYER + 4
CSTRIDE = 388
OSTRIDE = BS + 4
XSTRIDE = PART + 4
BIG = 1 << 20
MESH = pl.DeviceIdType.MESH
F32 = jnp.float32
BF16 = jnp.bfloat16
NT = (((1,), (1,)), ((), ()))
TN = (((0,), (0,)), ((), ()))


def iota(shape, dim):
    return lax.broadcasted_iota(jnp.int32, shape, dim)


def group_rows(block):
    return pl.ds(block * STRIDE, LAYER)


def of_position(position):
    return pl.ds(position, BS, stride=STRIDE)


def loop(count, unroll, body):
    def step(index, carry):
        for inner in range(unroll):
            body(index * unroll + inner)
        return carry

    lax.fori_loop(0, count // unroll, step, 0)


def relay_one(stage, targets, fine):
    for half in range(2):
        block = stage[:, fine, :, half * LAYER : (half + 1) * LAYER].reshape(128, LAYER)
        targets[half][group_rows(fine), :] = block.T.astype(F32)


def relay(stage, targets):
    loop(BS, 8, lambda fine: relay_one(stage, targets, fine))


def spread(rows_of, target):
    def body(fine):
        target[group_rows(fine), :] = jnp.concatenate(rows_of(fine), axis=0).T.astype(F32)

    loop(BS, 16, body)


def halves(ref, index):
    return ref[index, :, :LAYER], ref[index, :, LAYER:]


def left_of(sources, position):
    return jnp.concatenate(
        [source[of_position(position), :] for source in sources], axis=0
    ).astype(BF16)


def pick_plan(columns, device, far, near):
    count = columns.shape[1]
    partner = columns[1:2, :]
    row = iota((1, count), 1).astype(F32)
    value = partner.astype(F32)
    perm = (iota((count, count), 0) == partner - device * count).astype(BF16)
    order = iota((PART, count), 0)
    send, take = [], []
    for other in (far, near):
        there = (partner >= other * count) & (partner < (other + 1) * count)
        for entry, found in ((row, send), (value, take)):
            first = jnp.min(jnp.where(there, entry, float(BIG)), axis=1, keepdims=True)
            last = jnp.max(jnp.where(there, entry, -1.0), axis=1, keepdims=True)
            wanted = jnp.where(order == 0, first, jnp.where(order == 1, last, -2.0))
            hit = jnp.where(there, entry, -3.0) == wanted
            found.append(hit.astype(F32).astype(BF16))
    return perm, jnp.concatenate(send, axis=0), jnp.concatenate(take, axis=0)


def kernel(
    a_hbm, t_ref, s_ref, col_ref, pxl, xf, b2, b3,
    stage, b0, b1, b4, b5, b6, pn, yx, rr, other, pc, gath, below, above, own, s32, plan_perm, plan_send,
    plan_take, snd, rcv, in_sem, chunk_sem, send_sem, recv_sem,
):
    device = lax.axis_index("rows")
    part = lax.axis_index("cols")
    devices = lax.axis_size("rows")
    parts = lax.axis_size("cols")
    far = lax.rem(device + devices // 2, devices)
    near = device + 1 - 2 * lax.rem(device, 2)
    up = lax.rem(device + 1, devices)
    down = lax.rem(device + devices - 1, devices)
    right = lax.rem(part + 1, parts)
    left = lax.rem(part + parts - 1, parts)
    opposite = lax.rem(part + 2, parts)

    def fetch(pair, slot):
        return pltpu.make_async_copy(a_hbm.at[pl.ds(2 * pair, 2)], stage.at[slot], in_sem.at[slot])

    def send(source, target, index, to):
        return pltpu.make_async_remote_copy(
            src_ref=source, dst_ref=target, send_sem=send_sem.at[index],
            recv_sem=recv_sem.at[index], device_id=to, device_id_type=MESH,
        )

    def exchange(turn):
        return [
            send(snd.at[turn, kind], rcv.at[turn, kind], 2 * turn + kind, (who, part))
            for kind, who in ((0, far), (1, near))
        ]

    def first_fetch(chunk):
        rows = pl.ds(chunk * 16, 16)
        return pltpu.make_async_copy(
            a_hbm.at[pl.ds(0, 2), rows], stage.at[0, :, rows], chunk_sem.at[chunk]
        )

    for chunk in range(4):
        first_fetch(chunk).start()
    fetch(1, 1).start()
    barrier = pltpu.get_barrier_semaphore()
    for who in ((far, part), (up, part), (down, part), (device, right), (device, left)):
        pl.semaphore_signal(barrier, inc=1, device_id=who, device_id_type=MESH)

    perm, send_rows, take_rows = pick_plan(col_ref, device, far, near)
    plan_perm[...] = perm
    plan_send[...] = send_rows
    plan_take[...] = take_rows
    for half in range(2):
        s32[half] = s_ref[:, half * LAYER : (half + 1) * LAYER].astype(F32)

    def pack(turn, matrix):
        rows = lax.dot_general(plan_send[...], matrix, NT, preferred_element_type=F32).astype(BF16)
        snd[turn, 0] = rows[:PART]
        snd[turn, 1] = rows[PART:]

    def arrived(turn):
        rows = rcv[turn].reshape(2 * PART, -1)
        return lax.dot_general(rows, plan_take[...], TN, preferred_element_type=F32)

    pack(0, t_ref[...].reshape(BS * PART, 2 * LAYER))
    pl.semaphore_wait(barrier, 5)
    first = exchange(0)
    for copy in first:
        copy.start()

    for chunk in range(4):
        first_fetch(chunk).wait()
        loop(16, 8, lambda fine: relay_one(stage.at[0], (b0, b1), 16 * chunk + fine))
    fetch(2, 0).start()

    fetch(1, 1).wait()
    relay(stage.at[1], (b2, b3))
    fetch(3, 1).start()
    for copy in first:
        copy.wait()
    moved = jnp.dot(
        t_ref[...].reshape(BS * PART, 2 * LAYER), plan_perm[...], preferred_element_type=F32
    )
    other[...] = (moved + arrived(0)).astype(BF16).reshape(BS, PART, 2 * LAYER)

    tt, cp = yx, b6
    spread(lambda fine: [*halves(t_ref, fine), *halves(other, fine)] * 2, tt)

    lane = iota((1, 128), 1)
    mask = [((lane >= 32 * j) & (lane < 32 * j + 32)).astype(F32).astype(BF16) for j in range(4)]
    own_low = ((lane & 63) < 32).astype(F32).astype(BF16)
    own_high = ((lane & 63) >= 32).astype(F32).astype(BF16)
    first_layer = (iota((BS, 128), 1) & 16) == 0
    keep = ((iota((128, 128), 1) & 16) == 0) == (iota((128, 128), 0) < BS)

    def smooth(position):
        block = tt[of_position(position), :].astype(BF16)
        right_side = jnp.concatenate([block * own_low, block * own_high], axis=0)
        result = jnp.dot(left_of((b0, b1), position), right_side, preferred_element_type=F32)
        cp[of_position(position), :] = jnp.where(first_layer, result[:BS], result[BS:])

    loop(LAYER, 32, smooth)

    def back(pair):
        fine = 2 * pair
        joined = jnp.where(
            iota((LAYER, 128), 1) < 64, cp[group_rows(fine), :], cp[group_rows(fine + 1), :]
        ).T
        for step in range(2):
            for half in range(2):
                base = 64 * step + 16 * half
                coupled = joined[base : base + 16] + joined[base + 32 : base + 48]
                lanes = pl.ds(half * LAYER, LAYER)
                value = t_ref[fine + step, :, lanes].astype(F32)
                value = value - s32[half, pl.ds(fine + step, 1), :] * coupled
                value = value.astype(BF16)
                pxl[fine + step, :, lanes] = value
                rows = pl.ds((fine + step) * XSTRIDE, PART)
                xf[half, rows, :] = value.astype(F32)

    loop(BS // 2, 4, back)

    def swap(coarse):
        for half in range(2):
            rows = xf[half, pl.ds(coarse, BS, stride=XSTRIDE), :]
            pc[coarse, :, half * LAYER : (half + 1) * LAYER] = rows.astype(BF16)

    loop(PART, 4, swap)
    pack(1, pxl[...].reshape(BS * PART, 2 * LAYER))

    middle = PART // 2
    low = pl.ds(0, middle)
    high = pl.ds(middle, middle)
    first_half = [
        send(pc.at[low], gath.at[0, low], 6, (device, right)),
        send(pc.at[high], gath.at[1, high], 7, (device, left)),
    ]
    second_half = [
        send(pc.at[high], gath.at[0, high], 12, (device, right)),
        send(pc.at[low], gath.at[1, low], 13, (device, left)),
    ]
    relays = [
        send(gath.at[0, low], gath.at[2, low], 10, (device, right)),
        send(gath.at[1, high], gath.at[2, high], 11, (device, left)),
    ]
    halo = [
        send(pxl.at[:, :, pl.ds(LAYER, LAYER)], below, 8, (up, part)),
        send(pxl.at[:, :, pl.ds(0, LAYER)], above, 9, (down, part)),
    ]
    second = exchange(1)
    for copy in (*first_half, *second_half, *second, *halo):
        copy.start()

    spread(lambda fine: [*halves(pxl, fine)] * 4, yx)

    def settle(position):
        pn[position] = yx[of_position(position), :].astype(BF16)

    loop(LAYER, 16, settle)
    fetch(2, 0).wait()
    relay(stage.at[0], (b4, b5))
    fetch(3, 1).wait()

    def reach(slot, pairs, blocks, position):
        left_side = jnp.concatenate([left_of(pair, position) for pair in pairs], axis=1)
        right_side = jnp.concatenate([block * m for block, m in zip(blocks, mask)], axis=0)
        result = jnp.dot(left_side, right_side, preferred_element_type=F32)
        rr[slot, position] = jnp.where(keep, result, 0.0).astype(BF16)

    def local_line(line, carry):
        before = lax.rem(line + GY - 1, GY) * GX
        after = lax.rem(line + 1, GY) * GX
        base = line * GX
        for x in range(GX):
            blocks = [
                pn[base + (x + GX - 1) % GX], pn[base + (x + 1) % GX], pn[before + x], pn[after + x]
            ]
            reach(0, ((b2, b3), (b4, b5)), blocks, base + x)
        for inner in range(4):
            relay_one(stage.at[1], (b6, yx), line * 4 + inner)
        return carry

    def two_lines(index, carry):
        return local_line(2 * index + 1, local_line(2 * index, carry))

    def four_lines(index, carry):
        return two_lines(2 * index + 1, two_lines(2 * index, carry))

    lax.fori_loop(0, GY // 4, four_lines, 0)

    for copy in second:
        copy.wait()
    moved = jnp.dot(
        pxl[...].reshape(BS * PART, 2 * LAYER), plan_perm[...], preferred_element_type=F32
    )
    other[...] = (moved + arrived(1)).astype(BF16).reshape(BS, PART, 2 * LAYER)
    for copy in halo:
        copy.wait()

    def outer_rows(fine):
        low, high = halves(pxl, fine)
        return [low, high, *halves(other, fine), below[fine], low, high, above[fine]]

    spread(outer_rows, b2)
    for copy in first_half:
        copy.wait_recv()
    for copy in relays:
        copy.start()

    def remote_row(position):
        block = b2[of_position(position), :].astype(BF16)
        reach(1, ((b0, b1), (b6, yx)), [block] * 4, position)

    loop(LAYER, 32, remote_row)

    pf, off = b4, (b2, b3)

    def wide(source, index, place):
        def body(coarse):
            block = source[coarse] if index is None else source[index, coarse]
            rows = jnp.concatenate([block[:, :LAYER], block[:, LAYER:]], axis=0)
            pf[group_rows(place * PART + coarse), :] = rows.T.astype(F32)

        loop(PART, 16, body)

    def product(slots, start, count):
        def body(position):
            rows = pl.ds(start * STRIDE + position, count, stride=STRIDE)
            left_side = pf[rows, :].astype(BF16)
            right_side = [rr[slot, position] for slot in slots]
            right_side = right_side[0] if len(slots) == 1 else jnp.concatenate(right_side, axis=1)
            result = jnp.dot(left_side, right_side, preferred_element_type=F32)
            for order, slot in enumerate(slots):
                (b0, b1)[slot][rows, :] = result[:, order * 128 : (order + 1) * 128]

        loop(LAYER, 32, body)

    owners = (part, left, right, opposite)

    def keep_off(slot, half, coarse_row, rows):
        start = slot * BS + coarse_row
        off[half][pl.ds(start, PART, stride=CSTRIDE), :] = rows

    def finish_outer(place):
        def body(coarse):
            block = b1[group_rows(place * PART + coarse), :]
            coarse_row = owners[place] * PART + coarse
            high = block.astype(BF16)
            low = (block - high.astype(F32)).astype(BF16)
            turned = high.T.astype(F32)
            fixed = turned[:64] + low.T[:64].astype(F32)
            for half in range(2):
                base = 16 * half
                own[half, pl.ds(coarse_row, PART, stride=OSTRIDE), :] = (
                    fixed[base : base + 16] + fixed[base + 32 : base + 48]
                )
                keep_off(4, half, coarse_row, turned[base + 64 : base + 80])
                keep_off(5, half, coarse_row, turned[base + 96 : base + 112])

        loop(PART, 16, body)

    wide(pc, None, 0)
    for copy in first_half:
        copy.wait_send()
    for copy in second_half:
        copy.wait()
    wide(gath, 0, 1)
    wide(gath, 1, 2)
    product((0, 1), 0, 3 * PART)
    for place in range(3):
        finish_outer(place)
    for copy in relays:
        copy.wait()
    wide(gath, 2, 3)
    product((1,), 3 * PART, PART)
    finish_outer(3)

    def own_rows():
        return jnp.concatenate(
            [
                jnp.concatenate(
                    [own[half, pl.ds(c * OSTRIDE, BS), :] for c in range(PART)], axis=0
                )
                for half in range(2)
            ],
            axis=1,
        )

    high = own_rows().astype(BF16)
    pack(2, high)
    third = exchange(2)
    for copy in third:
        copy.start()

    product((0,), 3 * PART, PART)

    def finish_local(place):
        def body(coarse):
            turned = b0[group_rows(place * PART + coarse), :].astype(BF16).T.astype(F32)
            coarse_row = owners[place] * PART + coarse
            for half in range(2):
                for j in range(4):
                    base = 32 * j + 16 * half
                    keep_off(j, half, coarse_row, turned[base : base + 16])

        loop(PART, 16, body)

    for place in range(4):
        finish_local(place)
    whole = own_rows()
    high = whole.astype(BF16)
    low = (whole - high.astype(F32)).astype(BF16)
    total = whole + jnp.dot(high, plan_perm[...], preferred_element_type=F32)
    total = total + jnp.dot(low, plan_perm[...], preferred_element_type=F32)
    for copy in third:
        copy.wait()
    total = total + arrived(2)
    for half in range(2):
        xf[half, pl.ds(0, PART * BS), :] = total[:, half * LAYER : (half + 1) * LAYER]


def finish(p_ref, d_ref, low_ref, high_ref, p_out, d_out, o_out, planes, sems):
    early = [pltpu.make_async_copy(p_ref, p_out, sems.at[0])] + [
        pltpu.make_async_copy(
            d_ref.at[half, pl.ds(0, PART * BS)],
            d_out.at[:, pl.ds(half * LAYER, LAYER)],
            sems.at[1 + half],
        )
        for half in range(2)
    ]
    for copy in early:
        copy.start()
    late = []
    for chunk in range(4):

        def narrow(step):
            coarse = 4 * chunk + step
            for slot in range(6):
                for half, source in enumerate((low_ref, high_ref)):
                    rows = source[pl.ds(coarse * CSTRIDE + slot * BS, BS), :]
                    planes[coarse * 6 + slot, :, half * LAYER : (half + 1) * LAYER] = rows.astype(BF16)

        loop(4, 1, narrow)
        there = pl.ds(24 * chunk, 24)
        late.append(pltpu.make_async_copy(planes.at[there], o_out.at[there], sems.at[3 + chunk]))
        late[-1].start()
    for copy in (*early, *late):
        copy.wait()


def on_device(operator_blocks, tentative, jacobi_scale, columns):
    rows = columns.shape[1]
    vmem = pl.BlockSpec(memory_space=pltpu.VMEM)
    hbm = pl.BlockSpec(memory_space=pl.ANY)
    kept = pl.pallas_call(
        kernel,
        out_shape=(
            pltpu.VMEM((BS, PART, rows), BF16),
            pltpu.VMEM((2, BS * XSTRIDE, LAYER), F32),
            pltpu.VMEM((BS * STRIDE, 128), F32),
            pltpu.VMEM((BS * STRIDE, 128), F32),
        ),
        in_specs=[hbm, vmem, vmem, vmem],
        out_specs=(vmem,) * 4,
        scratch_shapes=[
            pltpu.VMEM((2, 2, BS, BS, rows), BF16),
            *[pltpu.VMEM((BS * STRIDE, 128), F32) for _ in range(5)],
            pltpu.VMEM((LAYER, BS, 128), BF16),
            pltpu.VMEM((BS * STRIDE, 128), F32),
            pltpu.VMEM((2, LAYER, 128, 128), BF16),
            pltpu.VMEM((BS, PART, rows), BF16),
            pltpu.VMEM((PART, BS, rows), BF16),
            pltpu.VMEM((3, PART, BS, rows), BF16),
            pltpu.VMEM((BS, PART, LAYER), BF16),
            pltpu.VMEM((BS, PART, LAYER), BF16),
            pltpu.VMEM((2, PART * OSTRIDE, LAYER), F32),
            pltpu.VMEM((2, BS, LAYER), F32),
            pltpu.VMEM((rows, rows), BF16),
            pltpu.VMEM((2 * PART, rows), BF16),
            pltpu.VMEM((2 * PART, rows), BF16),
            pltpu.VMEM((3, 2, PART, BS * PART), BF16),
            pltpu.VMEM((3, 2, PART, BS * PART), BF16),
            pltpu.SemaphoreType.DMA((2,)),
            pltpu.SemaphoreType.DMA((4,)),
            pltpu.SemaphoreType.DMA((14,)),
            pltpu.SemaphoreType.DMA((14,)),
        ],
        compiler_params=pltpu.CompilerParams(
            collective_id=0, has_side_effects=True, vmem_limit_bytes=51 * 2**20
        ),
    )(operator_blocks, tentative, jacobi_scale, columns)
    prolongator, diag, off = pl.pallas_call(
        finish,
        out_shape=(
            jax.ShapeDtypeStruct((BS, PART, rows), BF16),
            jax.ShapeDtypeStruct((PART * BS, rows), F32),
            jax.ShapeDtypeStruct((PART * 6, BS, rows), BF16),
        ),
        in_specs=[vmem] * 4,
        out_specs=(hbm,) * 3,
        scratch_shapes=[
            pltpu.VMEM((PART * 6, BS, rows), BF16),
            pltpu.SemaphoreType.DMA((7,)),
        ],
        compiler_params=pltpu.CompilerParams(vmem_limit_bytes=8 * 2**20),
    )(*kept)
    return prolongator, diag.reshape(PART, BS, rows), off.reshape(PART, 6, BS, rows)


def solution(mesh):
    placed = (
        P(None, None, None, "rows"),
        P(None, "cols", "rows"),
        P(None, "rows"),
        P(None, "rows"),
    )
    return jax.shard_map(
        on_device,
        mesh=mesh,
        in_specs=placed,
        out_specs=(P(None, "cols", "rows"), P("cols", None, "rows"), P("cols", None, None, "rows")),
        check_vma=False,
    )
```
